256 devices in a mesh: seq: 32 (over z, x), head: 8 (over y, core).
Axes of the slice: x: 4, y: 4, z: 8, core: 2. Of those that a mesh axis runs over, the one named last changes fastest.
Arguments:
- block_input: bfloat16 [8, 256, 5120], P(None, 'seq'), may hold values from -6 to 6
- accepted: bfloat16 [8, 256, 5120], P(None, 'seq'), may hold values from -6 to 6
- accept_mask: int32 [8, 256], P(None, 'seq'), may hold values 0 or 1
- cache_lengths: int32 [8], replicated, may hold values from 1 to 8192, as said below
- page_table: int32 [512], replicated, may hold values from 0 to 511, each once
- norm_gain: float32 [5120], replicated, may hold values from 0.1 to 1.9
- w_query: bfloat16 [5120, 3072], P('seq', 'head'), may hold values from -0.078125 to 0.078125
- w_key: bfloat16 [5120, 3072], P('seq', 'head'), may hold values from -0.078125 to 0.078125
- w_value: bfloat16 [5120, 3072], P('seq', 'head'), may hold values from -0.25 to 0.25
- w_out: bfloat16 [5120, 3072], P('seq', 'head'), may hold values from -0.109375 to 0.109375
- key_cache: bfloat16 [512, 128, 3072], P('seq', None, 'head')
- value_cache: bfloat16 [512, 128, 3072], P('seq', None, 'head'), may hold values from -18 to 18
Outputs:
- first_out: bfloat16 [8, 256, 5120], P(None, 'seq', 'head')
- second_out: bfloat16 [8, 256, 5120], P(None, 'seq', 'head')
The draws below stay inside these ranges and needn't reach their ends.
Inputs may be any that keep to these rules, and one draw needn't show every extreme that they name: `cache_lengths`: max(1, 4) requests, chosen at random, hold (63) * 128 + 1 to 8192 cached tokens, one of them exactly 8192; the others hold 1 to 256. `page_table`: A permutation of the 512 pool pages; entry r * 64 + j is the pool page of cached positions j * 128 to (j + 1) * 128 - 1 of request r.
All inputs are finite; a program needn't handle non-finite values. No bound on the sum of `accept_mask` on one device may be relied on, other than what follows from the above.
Results may differ from the reference program's by a relative error of at most 0.024.
The reference program's roundings to bfloat16 on the way count: a program that leaves them out, or rounds other values in their place, can miss the bound.
Values may be sent and summed in bfloat16 or wider, within the bound.
A program may use at most 128 MiB of HBM per device.

```python
import jax
import jax.numpy as jnp
from jax import lax

D = 5120
HD = 128
HEADS = 24
BLOCK = 256
PAGE = 128
MAXP = 64
REQ = 8
POOL = 512


def draw_key_cache(key, part):
    noise_key = jax.random.fold_in(key, 0)
    samples = jnp.clip(jax.random.normal(noise_key, (POOL, PAGE, HEADS * HD), jnp.float32), -6.0, 6.0)
    return samples.astype(jnp.bfloat16)


def draw_cache_lengths(key, part):
    order_key, long_key, short_key = jax.random.split(key, 3)
    order = jax.random.permutation(order_key, REQ)
    ranking = jnp.argsort(order)
    longer = ranking < max(REQ // 2, 1)
    long_length = MAXP * PAGE - jax.random.randint(long_key, (REQ,), 0, PAGE)
    long_length = jnp.where(ranking == 0, MAXP * PAGE, long_length)
    short_length = jax.random.randint(short_key, (REQ,), 1, 2 * PAGE + 1)
    return jnp.where(longer, long_length, short_length).astype(jnp.int32)


def plant(result, stream_key, low, top_value):
    spot = [jax.random.randint(jax.random.fold_in(stream_key, axis), (), 0, length) for axis, length in enumerate(result.shape)]
    longest = result.shape.index(max(result.shape))
    beside = spot[:longest] + [(spot[longest] + 1) % result.shape[longest]] + spot[longest + 1:]
    return result.at[tuple(spot)].set(low).at[tuple(beside)].set(top_value)


def block_scale(stream_key, extent, shards, low, largest):
    factor_of, own = 1.0, jax.random.fold_in(stream_key, 6)
    for dim, parts in shards:
        heights = jnp.exp(jax.random.uniform(jax.random.fold_in(own, dim), (parts,), jnp.float32, low / len(shards), largest / len(shards)))
        factor_of = factor_of * jnp.repeat(heights, extent[dim] // parts).reshape([-1 if axis == dim else 1 for axis in range(len(extent))])
    return factor_of


def bell_draw(stream_key, extent, width, bound, cuts=(), kind=jnp.bfloat16):
    array = jax.random.normal(stream_key, extent, jnp.float32) * width
    if len(cuts) > 0:
        array = block_scale(stream_key, extent, cuts, -0.22, 0.18) * array
    return jnp.clip(array, min=-bound, max=bound).astype(kind)


def setup_inputs(seed: int = 0) -> dict:
    keys = jax.random.split(jax.random.key(seed), 13)
    return {
        "block_input": bell_draw(keys[0], (REQ, BLOCK, D), 1.0, 6.0, ((1, 32),)),
        "accepted": bell_draw(keys[1], (REQ, BLOCK, D), 1.0, 6.0, ((1, 32),)),
        "accept_mask": plant((jax.random.randint(keys[2], (REQ, BLOCK), 0, 2) < 1).astype(jnp.int32), jax.random.fold_in(keys[2], 1), 0, 1),
        "cache_lengths": draw_cache_lengths(jax.random.fold_in(keys[12], 71), 0),
        "page_table": jax.random.permutation(keys[4], POOL).astype(jnp.int32),
        "norm_gain": jnp.clip(1.0 + 0.18 * jax.random.normal(keys[5], (D,), jnp.float32), 0.1, 1.9),
        "w_query": bell_draw(keys[6], (D, HEADS * HD), D ** -0.5, 0.078125, ((0, 32), (1, 8))),
        "w_key": bell_draw(keys[7], (D, HEADS * HD), D ** -0.5, 0.078125, ((0, 32), (1, 8))),
        "w_value": bell_draw(keys[8], (D, HEADS * HD), (D // 9) ** -0.5, 0.25, ((0, 32), (1, 8))),
        "w_out": bell_draw(keys[9], (D, HEADS * HD), (HEADS * HD) ** -0.5, 0.109375, ((0, 32), (1, 8))),
        "key_cache": draw_key_cache(jax.random.fold_in(keys[12], 71), 0),
        "value_cache": bell_draw(keys[11], (POOL, PAGE, HEADS * HD), 3.0, 18.0, ((0, 32), (2, 8))),
    }


masked_score = -1e+30

def rotate(vectors, positions):
    half_width = vectors.shape[-1] // 2
    frequency = 10000.0 ** (-(jnp.arange(half_width).astype(jnp.float32) * 2.0) / vectors.shape[-1])
    angles = positions[..., None, None] * frequency
    cosine = jnp.cos(angles)
    sine_part = jnp.sin(angles)
    front_half = vectors[..., :half_width]
    back_half = vectors[..., half_width:]
    return jnp.concatenate([front_half * cosine - back_half * sine_part, back_half * cosine + front_half * sine_part], axis=-1)

def normalize(inputs, norm_gain):
    widened = inputs.astype(jnp.float32)
    inverse = lax.rsqrt(lax.optimization_barrier(jnp.mean(widened * widened, axis=-1, keepdims=True)) + 1e-05)
    return (widened * inverse * norm_gain).astype(jnp.bfloat16)

def one_pass(inputs, cache_lengths, page_table, norm_gain, w_query, w_key, w_value, w_out, key_cache, value_cache):
    token_rows = normalize(inputs, norm_gain).reshape(REQ * BLOCK, D)
    positions = (cache_lengths[:, None] + jnp.arange(BLOCK, dtype=jnp.int32)[None, :]).astype(jnp.float32)
    shaped = (REQ, BLOCK, HEADS, HD)
    queries = rotate(jnp.dot(token_rows, w_query, preferred_element_type=jnp.float32).reshape(shaped), positions).astype(jnp.bfloat16)
    new_keys = rotate(jnp.dot(token_rows, w_key, preferred_element_type=jnp.float32).reshape(shaped), positions).astype(jnp.bfloat16)
    new_values = jnp.dot(token_rows, w_value, preferred_element_type=jnp.float32).reshape(shaped).astype(jnp.bfloat16)
    page_rows = page_table.reshape(REQ, MAXP)

    def attend(request):
        block_queries, block_keys, block_values, page_ids, length = request
        wide_queries = block_queries.astype(jnp.float32)
        cached_keys = jnp.take(key_cache, page_ids, axis=0).reshape(MAXP * PAGE, HEADS, HD).astype(jnp.float32)
        cached_values = jnp.take(value_cache, page_ids, axis=0).reshape(MAXP * PAGE, HEADS, HD).astype(jnp.float32)
        key_live = jnp.arange(MAXP * PAGE, dtype=jnp.int32) < length
        cache_scores = jnp.einsum('qhd,khd->qhk', wide_queries, cached_keys) * HD ** (-0.5)
        cache_scores = jnp.where(key_live, cache_scores, masked_score)
        block_scores = jnp.einsum('qhd,khd->qhk', wide_queries, block_keys.astype(jnp.float32)) * HD ** (-0.5)
        row_peak = jnp.maximum(lax.optimization_barrier(jnp.max(cache_scores, axis=-1)), lax.optimization_barrier(jnp.max(block_scores, axis=-1)))
        paged = cache_scores.reshape(BLOCK, HEADS, MAXP, PAGE)
        paged_live = key_live.reshape(MAXP, PAGE)
        page_peak = lax.optimization_barrier(jnp.max(paged, axis=-1))
        page_weights = jnp.where(paged_live, jnp.exp(paged - page_peak[..., None]), 0.0)
        factor = jnp.exp(page_peak - row_peak[..., None])
        rounded = lax.optimization_barrier(page_weights.astype(jnp.bfloat16)).astype(jnp.float32)
        scaled = (rounded * factor[..., None]).reshape(BLOCK, HEADS, MAXP * PAGE)
        cache_total = lax.optimization_barrier(jnp.sum(page_weights * factor[..., None], axis=(-2, -1)))
        block_weights = jnp.exp(block_scores - row_peak[..., None])
        weight_total = cache_total + lax.optimization_barrier(jnp.sum(block_weights, axis=-1))
        weighted = jnp.einsum('qhk,khd->qhd', scaled, cached_values) + jnp.einsum('qhk,khd->qhd', block_weights, block_values.astype(jnp.float32))
        return (weighted / weight_total[..., None]).astype(jnp.bfloat16)
    context = lax.map(attend, (queries, new_keys, new_values, page_rows, cache_lengths))
    context_rows = context.reshape(REQ * BLOCK, HEADS * HD)
    projected = lax.dot_general(context_rows, w_out, (((1,), (1,)), ((), ())), preferred_element_type=jnp.float32)
    return projected.astype(jnp.bfloat16).reshape(REQ, BLOCK, D)

def reference(block_input, accepted, accept_mask, cache_lengths, page_table, norm_gain, w_query, w_key, w_value, w_out, key_cache, value_cache):
    first_out = one_pass(block_input, cache_lengths, page_table, norm_gain, w_query, w_key, w_value, w_out, key_cache, value_cache)
    swapped = jnp.where(accept_mask[:, :, None] == 1, accepted, block_input)
    second_out = one_pass(swapped, cache_lengths, page_table, norm_gain, w_query, w_key, w_value, w_out, key_cache, value_cache)
    return (first_out, second_out)
```

```python
import functools

import jax
import jax.numpy as jnp
from jax import lax
from jax.experimental import pallas as pl
from jax.experimental.pallas import tpu as pltpu
from jax.sharding import PartitionSpec as P

HD = 128
PAGE = 128
MAXP = 64
X = 4
BLK = 160
COVER = 256
MESH = pl.DeviceIdType.MESH
F32 = jnp.float32
BF16 = jnp.bfloat16
NT = (((1,), (1,)), ((), ()))
TN = (((0,), (0,)), ((), ()))


def place(Z):
    seq = lax.axis_index("seq")
    head = lax.axis_index("head")
    z, x = seq // X, lax.rem(seq, X)

    def at(dz, dx):
        return (lax.rem(z + dz + Z, Z) * X + lax.rem(x + dx, X), head)

    return seq, head, z, x, at


def greet(partners):
    barrier = pltpu.get_barrier_semaphore()
    for partner in partners:
        pl.semaphore_signal(barrier, inc=1, device_id=partner, device_id_type=MESH)
    pl.semaphore_wait(barrier, len(partners))


def remote(src, dst, send, recv, target):
    return pltpu.make_async_remote_copy(
        src_ref=src, dst_ref=dst, send_sem=send, recv_sem=recv, device_id=target, device_id_type=MESH
    )


def project_kernel(
    Z,
    x_ref,
    a_ref,
    mask_ref,
    gain_ref,
    cos_ref,
    sin_ref,
    wq_ref,
    wk_ref,
    wv_ref,
    wo_ref,
    q_all,
    kn_ref,
    vn_ref,
    wo_all,
    xn,
    xg,
    wb,
    acc,
    part,
    got,
    qloc,
    ring_send,
    ring_recv,
    tok_send,
    tok_recv,
    part_send,
    part_recv,
    zq_send,
    zq_recv,
    xq_send,
    xq_recv,
    local_sem,
):
    seq, head, z, x, at = place(Z)
    width = X * BLK
    off = pl.multiple_of(32 * x, 32)
    own = (wq_ref, wk_ref, wv_ref, wo_ref)
    greet([at(d, 0) for d in range(1, Z)] + [at(0, d) for d in range(1, X)])

    def ring(right, t, k):
        block = lax.rem(z - k + Z, Z) if right else lax.rem(z + k, Z)
        slot = wo_all.at[block] if t == 3 else wb.at[t, block, pl.ds(off, BLK)]
        src = own[t] if k == 0 else slot
        way = 1 if right else 0
        return remote(
            src, slot, ring_send.at[way, t, k], ring_recv.at[way, t, k], at(1 if right else -1, 0)
        )

    def steps(t, right):
        return Z // 2 if right == (t % 2 == 0) else Z - 1 - Z // 2

    def advance(tensors, k):
        for t in tensors:
            for right in (True, False):
                if 0 < k <= steps(t, right):
                    ring(right, t, k - 1).wait_recv()
                if k < steps(t, right):
                    ring(right, t, k).start()

    advance((0, 1), 0)
    own_out = pltpu.make_async_copy(wo_ref, wo_all.at[z], local_sem.at[0])
    own_out.start()

    @pl.loop(0, x_ref.shape[0])
    def _(r):
        first = x_ref[r].astype(F32)
        second = jnp.where(mask_ref[r] == 1, a_ref[r].astype(F32), first)
        both = jnp.concatenate([first, second], axis=0)
        inverse = lax.rsqrt(jnp.mean(both * both, axis=-1, keepdims=True) + 1e-05)
        normed = (both * inverse * gain_ref[...]).astype(BF16)
        rows = pl.ds(pl.multiple_of(r * 16, 16), 16)
        for c in range(Z):
            xn[c, rows, :] = normed[:, c * width : (c + 1) * width]

    mine = pl.ds(pl.multiple_of(x * 128, 128), 128)
    tokens = []
    for d in range(1, X):
        there = lax.rem(x + d, X)
        copy = remote(
            xn.at[:, :, pl.ds(pl.multiple_of(there * 128, 128), COVER)],
            xg.at[:, mine],
            tok_send.at[d - 1],
            tok_recv.at[d - 1],
            at(0, d),
        )
        copy.start()
        tokens.append(copy)
    own_tokens = pltpu.make_async_copy(xn.at[:, :, pl.ds(pl.multiple_of(x * 128, 128), COVER)], xg.at[:, mine], local_sem.at[1])
    own_tokens.start()

    advance((0, 1), 1)

    zero = jnp.zeros((32, wb.shape[3]), BF16)

    @pl.loop(0, Z)
    def _(c):
        for t in range(3):
            for j in range(3):
                stripe = pl.multiple_of(32 * lax.rem(x + 5 + j, 8), 32)
                wb[t, c, pl.ds(stripe, 32), :] = zero

    for t in range(3):
        wb[t, z, pl.ds(off, BLK), :] = own[t][...]

    advance((0, 1), 2)
    advance((0, 1), 3)
    advance((2, 3), 0)
    advance((0, 1), 4)
    own_tokens.wait()
    for copy in tokens:
        copy.wait_recv()

    def multiply(t):
        acc[t] = jnp.zeros(acc.shape[1:], F32)

        @pl.loop(0, Z)
        def _(c):
            acc[t] += jnp.dot(xg[c], wb[t, c], preferred_element_type=F32)

        copies = []
        for d in range(1, X):
            there = lax.rem(x + d, X)
            part[t, d - 1] = acc[t, pl.ds(pl.multiple_of(there * 128, 128), 128), :].astype(BF16)
            copy = remote(
                part.at[t, d - 1], got.at[t, d - 1], part_send.at[t, d - 1], part_recv.at[t, d - 1], at(0, d)
            )
            copy.start()
            copies.append(copy)
        return copies

    def collect(t, copies):
        total = acc[t, mine, :]
        for copy in copies:
            copy.wait_recv()
        for d in range(1, X):
            total = total + got[t, d - 1].astype(F32)
        return total

    def turn(rows):
        pieces = []
        for h in range(rows.shape[1] // HD):
            piece = rows[:, h * HD : (h + 1) * HD]
            pieces.append(piece * cos_ref[...] + pltpu.roll(piece, HD // 2, 1) * sin_ref[...])
        return jnp.concatenate(pieces, axis=1).astype(BF16)

    q_copies = multiply(0)
    k_copies = multiply(1)
    advance((2, 3), 1)
    query = turn(collect(0, q_copies))
    for r in range(qloc.shape[0]):
        qloc[r] = query[r * 16 : (r + 1) * 16]
    own_query = pltpu.make_async_copy(qloc, q_all.at[:, seq], local_sem.at[2])
    own_query.start()

    def to_z(d):
        return remote(qloc, q_all.at[:, seq], zq_send.at[d - 1], zq_recv.at[d - 1], at(d, 0))

    def to_x(dz, d):
        slot = q_all.at[:, lax.rem(z - dz + Z, Z) * X + x]
        return remote(qloc if dz == 0 else slot, slot, xq_send.at[d - 1, dz], xq_recv.at[d - 1, dz], at(0, d))

    arrival = sorted(range(1, Z), key=lambda d: min(d, Z - d))
    for d in arrival:
        to_z(d).start()
    for d in range(1, X):
        to_x(0, d).start()
    advance((2, 3), 2)
    kn_ref[...] = turn(collect(1, k_copies))
    advance((2, 3), 3)
    for d in arrival[: Z // 2]:
        to_z(d).wait_recv()
        for e in range(1, X):
            to_x(d, e).start()
    advance((2, 3), 4)
    v_copies = multiply(2)
    for d in arrival[Z // 2 :]:
        to_z(d).wait_recv()
        for e in range(1, X):
            to_x(d, e).start()
    vn_ref[...] = collect(2, v_copies).astype(BF16)

    own_out.wait()
    own_query.wait()
    for t in range(4):
        for right in (True, False):
            for k in range(steps(t, right)):
                ring(right, t, k).wait_send()
    for copy in tokens + q_copies + k_copies + v_copies:
        copy.wait_send()
    for d in range(1, Z):
        to_z(d).wait_send()
    for dz in range(Z):
        for d in range(1, X):
            to_x(dz, d).wait()


def project(Z, block_input, accepted, mask, gain, cosine, sine, w_query, w_key, w_value, w_out):
    requests = block_input.shape[0]
    cols = w_query.shape[1]
    rows = requests * 16
    vmem = pl.BlockSpec(memory_space=pltpu.VMEM)
    hbm = pl.BlockSpec(memory_space=pl.ANY)
    dma = pltpu.SemaphoreType.DMA
    return pl.pallas_call(
        functools.partial(project_kernel, Z),
        name="project",
        out_shape=(
            jax.ShapeDtypeStruct((requests, Z * X, 16, cols), BF16),
            jax.ShapeDtypeStruct((rows, cols), BF16),
            jax.ShapeDtypeStruct((rows, cols), BF16),
            jax.ShapeDtypeStruct((Z, BLK, cols), BF16),
        ),
        in_specs=[vmem] * 10,
        out_specs=(hbm, vmem, vmem, hbm),
        scratch_shapes=[
            pltpu.VMEM((Z, rows, X * BLK), BF16),
            pltpu.VMEM((Z, X * rows, COVER), BF16),
            pltpu.VMEM((3, Z, COVER, cols), BF16),
            pltpu.VMEM((3, X * rows, cols), F32),
            pltpu.VMEM((3, X - 1, rows, cols), BF16),
            pltpu.VMEM((3, X - 1, rows, cols), BF16),
            pltpu.VMEM((requests, 16, cols), BF16),
            dma((2, 4, Z // 2)),
            dma((2, 4, Z // 2)),
            dma((X - 1,)),
            dma((X - 1,)),
            dma((3, X - 1)),
            dma((3, X - 1)),
            dma((Z - 1,)),
            dma((Z - 1,)),
            dma((X - 1, Z)),
            dma((X - 1, Z)),
            dma((3,)),
        ],
        compiler_params=pltpu.CompilerParams(
            collective_id=0, has_side_effects=True, vmem_limit_bytes=44 << 20
        ),
    )(block_input, accepted, mask, gain, cosine, sine, w_query, w_key, w_value, w_out)


def attend_kernel(owner, live, q_ref, k_ref, v_ref, kn_ref, vn_ref, o_ref, st_ref, acc, stats):
    r = pl.program_id(0)
    heads = acc.shape[0]
    queries = acc.shape[2]
    scale = HD ** (-0.5)

    @pl.when(r == 0)
    def _():
        stats[...] = jnp.zeros_like(stats)

    key_pass = lax.broadcasted_iota(jnp.int32, (16, queries), 0) // 8
    query_pass = lax.rem(lax.broadcasted_iota(jnp.int32, (16, queries), 1) // 8, 2)
    same = key_pass == query_pass
    for h in range(heads):
        col = slice(h * HD, (h + 1) * HD)
        scores = lax.dot_general(kn_ref[0, :, col], q_ref[0, :, col], NT, preferred_element_type=F32) * scale
        scores = jnp.where(same, scores, -1e30)
        peak = jnp.max(scores, axis=0, keepdims=True)
        weights = jnp.where(same, jnp.exp(scores - peak), 0.0)
        high = weights.astype(BF16)
        low = (weights - high.astype(F32)).astype(BF16)
        values = vn_ref[0, :, col]
        acc[h] = lax.dot_general(
            jnp.concatenate([values, values], axis=0),
            jnp.concatenate([high, low], axis=0),
            TN,
            preferred_element_type=F32,
        )
        stats[pl.ds(r * 8 + h, 1), :] = peak
        stats[pl.ds(r * 8 + 4 + h, 1), :] = jnp.sum(weights, axis=0, keepdims=True)

    slot = lax.broadcasted_iota(jnp.int32, (PAGE, queries), 0)

    @pl.loop(0, k_ref.shape[0])
    def _(p):
        @pl.when(jnp.logical_and(owner[p] == r, live[p] > 0))
        def _():
            alive = slot < live[p]
            for h in range(heads):
                col = slice(h * HD, (h + 1) * HD)
                scores = lax.dot_general(k_ref[p, :, col], q_ref[0, :, col], NT, preferred_element_type=F32) * scale
                scores = jnp.where(alive, scores, -1e30)
                page_peak = jnp.max(scores, axis=0, keepdims=True)
                weights = jnp.where(alive, jnp.exp(scores - page_peak), 0.0)
                page_out = lax.dot_general(
                    v_ref[p, :, col], weights.astype(BF16), TN, preferred_element_type=F32
                )
                m_row = pl.ds(r * 8 + h, 1)
                l_row = pl.ds(r * 8 + 4 + h, 1)
                before = stats[m_row, :]
                after = jnp.maximum(before, page_peak)
                old, new = jnp.exp(before - after), jnp.exp(page_peak - after)
                acc[h] = acc[h] * old + page_out * new
                stats[m_row, :] = after
                stats[l_row, :] = stats[l_row, :] * old + jnp.sum(weights, axis=0, keepdims=True) * new

    for h in range(heads):
        o_ref[0, :, h * HD : (h + 1) * HD] = jnp.transpose(acc[h]).astype(BF16)

    @pl.when(r == pl.num_programs(0) - 1)
    def _():
        st_ref[...] = jnp.transpose(stats[...])


def attend(owner, live, q_all, key_cache, value_cache, new_keys, new_values):
    requests, queries, cols = q_all.shape
    pages = key_cache.shape[0]
    heads = cols // HD
    return pl.pallas_call(
        attend_kernel,
        name="attend",
        out_shape=(
            jax.ShapeDtypeStruct((requests, queries, cols), BF16),
            jax.ShapeDtypeStruct((queries, 128), F32),
        ),
        grid_spec=pltpu.PrefetchScalarGridSpec(
            num_scalar_prefetch=2,
            grid=(requests,),
            in_specs=[
                pl.BlockSpec((1, queries, cols), lambda r, *_: (r, 0, 0)),
                pl.BlockSpec((pages, PAGE, cols), lambda r, *_: (0, 0, 0)),
                pl.BlockSpec((pages, PAGE, cols), lambda r, *_: (0, 0, 0)),
                pl.BlockSpec((1, 16, cols), lambda r, *_: (r, 0, 0)),
                pl.BlockSpec((1, 16, cols), lambda r, *_: (r, 0, 0)),
            ],
            out_specs=[
                pl.BlockSpec((1, queries, cols), lambda r, *_: (r, 0, 0)),
                pl.BlockSpec((queries, 128), lambda r, *_: (0, 0)),
            ],
            scratch_shapes=[
                pltpu.VMEM((heads, HD, queries), F32),
                pltpu.VMEM((128, queries), F32),
            ],
        ),
        compiler_params=pltpu.CompilerParams(vmem_limit_bytes=40 << 20),
    )(owner, live, q_all, key_cache, value_cache, new_keys, new_values)


def join(tables, pieces, emit):
    peak = functools.reduce(jnp.maximum, tables)
    factors = [jnp.exp(table - peak) for table in tables]
    shifted = [pltpu.roll(factor, 4, 1) for factor in factors]
    total = sum(s * table for s, table in zip(shifted, tables))
    lane = lax.broadcasted_iota(jnp.int32, peak.shape, 1)
    table = jnp.where(lax.rem(lane, 8) >= 4, total, peak)
    emit(table, factors)


def finish_kernel(
    Z,
    o_ref,
    st_ref,
    wo_ref,
    first_ref,
    second_ref,
    oown,
    ra,
    ra_st,
    cb,
    cb_st,
    rb,
    rb_st,
    ctx,
    pb,
    ph,
    ob,
    of,
    a_send,
    a_recv,
    as_send,
    as_recv,
    b_send,
    b_recv,
    bs_send,
    bs_recv,
    c_send,
    c_recv,
    d_send,
    d_recv,
    e_send,
    e_recv,
    local_sem,
):
    seq, head, z, x, at = place(Z)
    requests = oown.shape[0]
    heads = oown.shape[3] // HD

    def other(d):
        return (seq, lax.rem(head + d, Z))

    greet(
        [at(d, 0) for d in range(1, Z)]
        + [at(0, d) for d in range(1, X)]
        + [other(d) for d in range(1, Z)]
    )

    def to_x(zi, d):
        there = lax.rem(z + zi, Z)
        return remote(
            o_ref.at[:, there, lax.rem(x + d, X)],
            ra.at[d - 1, there],
            a_send.at[d - 1, zi],
            a_recv.at[d - 1, zi],
            at(0, d),
        )

    def to_x_st(d):
        return remote(
            st_ref.at[:, lax.rem(x + d, X)], ra_st.at[d - 1], as_send.at[d - 1], as_recv.at[d - 1], at(0, d)
        )

    own = pltpu.make_async_copy(o_ref.at[:, :, x], oown, local_sem.at[0])
    own.start()
    for d in range(1, X):
        to_x_st(d).start()

    @pl.loop(1, Z + 1)
    def _(i):
        zi = lax.rem(i, Z)
        for d in range(1, X):
            to_x(zi, d).start()

    own.wait()
    for d in range(1, X):
        to_x_st(d).wait_recv()

    def to_z(zi):
        there = lax.rem(z + zi, Z)
        target = (there * X + x, head)
        return (
            remote(cb.at[there], rb.at[zi - 1], b_send.at[zi - 1], b_recv.at[zi - 1], target),
            remote(cb_st.at[there], rb_st.at[zi - 1], bs_send.at[zi - 1], bs_recv.at[zi - 1], target),
        )

    def gather_x(zi):
        there = lax.rem(z + zi, Z)
        for d in range(1, X):
            to_x(zi, d).wait_recv()
        tables = [st_ref[there, x]] + [ra_st[d - 1, there] for d in range(1, X)]

        def emit(table, factors):
            cb_st[there] = table
            for r in range(requests):
                sources = [oown[r, there]] + [ra[d - 1, there, r] for d in range(1, X)]
                for h in range(heads):
                    col = slice(h * HD, (h + 1) * HD)
                    lane = r * 8 + h
                    value = sum(
                        factor[:, lane : lane + 1] * source[:, col].astype(F32)
                        for factor, source in zip(factors, sources)
                    )
                    cb[there, r, :, col] = value.astype(BF16)

        join(tables, None, emit)

    @pl.loop(1, Z)
    def _(zi):
        gather_x(zi)
        for copy in to_z(zi):
            copy.start()

    gather_x(0)
    for d in range(1, Z):
        for copy in to_z(d):
            copy.wait_recv()

    mine = pl.multiple_of(x * 128, 128)

    def emit(table, factors):
        inverse = 1.0 / table
        for r in range(requests):
            sources = [cb[z, r]] + [rb[d - 1, r] for d in range(1, Z)]
            for h in range(heads):
                col = slice(h * HD, (h + 1) * HD)
                lane = r * 8 + h
                value = sum(
                    factor[:, lane : lane + 1] * source[:, col].astype(F32)
                    for factor, source in zip(factors, sources)
                )
                value = value * inverse[:, lane + 4 : lane + 5]
                ctx[pl.ds(mine + r * 16, 16), col] = value.astype(BF16)

    join([cb_st[z]] + [rb_st[d - 1] for d in range(1, Z)], None, emit)

    rows = pl.ds(mine, 128)
    shares = [remote(ctx.at[rows], ctx.at[rows], c_send.at[d - 1], c_recv.at[d - 1], at(0, d)) for d in range(1, X)]
    for copy in shares:
        copy.start()
    for copy in shares:
        copy.wait_recv()

    def to_head(d):
        return remote(pb.at[d - 1], ph.at[d - 1], d_send.at[d - 1], d_recv.at[d - 1], other(d))

    def partial(d):
        return lax.dot_general(wo_ref[lax.rem(head + d, Z)], ctx[...], NT, preferred_element_type=F32)

    @pl.loop(1, Z)
    def _(d):
        pb[d - 1] = partial(d).astype(BF16)
        to_head(d).start()

    total = partial(0)
    for d in range(1, Z):
        to_head(d).wait_recv()
        total = total + ph[d - 1].astype(F32)
    ob[...] = total.astype(BF16)
    block = pl.ds(pl.multiple_of(x * BLK, 32), BLK)

    def to_owner(d):
        there = pl.multiple_of(lax.rem(x + d, X) * 128, 128)
        return remote(ob.at[:, pl.ds(there, 128)], of.at[block], e_send.at[d - 1], e_recv.at[d - 1], at(0, d))

    for d in range(1, X):
        to_owner(d).start()
    last = pltpu.make_async_copy(ob.at[:, pl.ds(mine, 128)], of.at[block], local_sem.at[1])
    last.start()
    last.wait()
    for d in range(1, X):
        to_owner(d).wait_recv()
    result = jnp.transpose(of[...].astype(F32))
    for r in range(requests):
        first_ref[r] = result[r * 16 : r * 16 + 8].astype(BF16)
        second_ref[r] = result[r * 16 + 8 : r * 16 + 16].astype(BF16)

    for d in range(1, X):
        to_x_st(d).wait_send()
        shares[d - 1].wait_send()
        to_owner(d).wait_send()

        @pl.loop(0, Z)
        def _(zi):
            to_x(zi, d).wait_send()

    for d in range(1, Z):
        for copy in to_z(d):
            copy.wait_send()
        to_head(d).wait_send()


def finish(Z, out, table, wo_all, tokens):
    requests = out.shape[0]
    cols = out.shape[4]
    rows = requests * 16
    vmem = pl.BlockSpec(memory_space=pltpu.VMEM)
    hbm = pl.BlockSpec(memory_space=pl.ANY)
    dma = pltpu.SemaphoreType.DMA
    shape = jax.ShapeDtypeStruct((requests, tokens, X * BLK), BF16)
    return pl.pallas_call(
        functools.partial(finish_kernel, Z),
        name="finish",
        out_shape=(shape, shape),
        in_specs=[hbm, vmem, vmem],
        out_specs=(vmem, vmem),
        scratch_shapes=[
            pltpu.VMEM((requests, Z, 16, cols), BF16),
            pltpu.VMEM((X - 1, Z, requests, 16, cols), BF16),
            pltpu.VMEM((X - 1, Z, 16, 128), F32),
            pltpu.VMEM((Z, requests, 16, cols), BF16),
            pltpu.VMEM((Z, 16, 128), F32),
            pltpu.VMEM((Z - 1, requests, 16, cols), BF16),
            pltpu.VMEM((Z - 1, 16, 128), F32),
            pltpu.VMEM((X * rows, cols), BF16),
            pltpu.VMEM((Z - 1, BLK, X * rows), BF16),
            pltpu.VMEM((Z - 1, BLK, X * rows), BF16),
            pltpu.VMEM((BLK, X * rows), BF16),
            pltpu.VMEM((X * BLK, rows), BF16),
            dma((X - 1, Z)),
            dma((X - 1, Z)),
            dma((X - 1,)),
            dma((X - 1,)),
            dma((Z - 1,)),
            dma((Z - 1,)),
            dma((Z - 1,)),
            dma((Z - 1,)),
            dma((X - 1,)),
            dma((X - 1,)),
            dma((Z - 1,)),
            dma((Z - 1,)),
            dma((X - 1,)),
            dma((X - 1,)),
            dma((2,)),
        ],
        compiler_params=pltpu.CompilerParams(
            collective_id=1, has_side_effects=True, vmem_limit_bytes=44 << 20
        ),
    )(out, table, wo_all)


def per_device(
    Z,
    block_input,
    accepted,
    accept_mask,
    cache_lengths,
    page_table,
    norm_gain,
    w_query,
    w_key,
    w_value,
    w_out,
    key_cache,
    value_cache,
):
    seq = lax.axis_index("seq")
    requests, tokens, width = block_input.shape
    half = HD // 2
    frequency = 10000.0 ** (-(jnp.arange(half).astype(F32) * 2.0) / HD)
    positions = (
        cache_lengths[:, None] + seq * tokens + jnp.arange(tokens, dtype=jnp.int32)[None, :]
    ).astype(F32)
    angles = jnp.broadcast_to(positions[:, None, :, None] * frequency, (requests, 2, tokens, half))
    angles = angles.reshape(requests * 2 * tokens, half)
    cosine, sine = jnp.cos(angles), jnp.sin(angles)
    cosine = jnp.concatenate([cosine, cosine], axis=1)
    sine = jnp.concatenate([-sine, sine], axis=1)

    pages_here = key_cache.shape[0]
    page_ids = seq * pages_here + jnp.arange(pages_here, dtype=jnp.int32)
    table_slots = jnp.arange(page_table.shape[0], dtype=jnp.int32)
    slot_of = jnp.sum(
        jnp.where(page_table[None, :] == page_ids[:, None], table_slots[None, :], 0), axis=1
    )
    owner = slot_of // MAXP
    owner_match = owner[:, None] == jnp.arange(requests, dtype=jnp.int32)[None, :]
    owner_length = jnp.sum(jnp.where(owner_match, cache_lengths[None, :], 0), axis=1)
    live = owner_length - (slot_of % MAXP) * PAGE

    q_all, new_keys, new_values, wo_all = project(
        Z,
        block_input,
        accepted,
        accept_mask.reshape(requests, tokens, 1),
        norm_gain.reshape(1, width),
        cosine,
        sine,
        w_query,
        w_key,
        w_value,
        w_out,
    )
    cols = q_all.shape[3]
    queries = Z * X * 16
    out, table = attend(
        owner,
        live,
        q_all.reshape(requests, queries, cols),
        key_cache,
        value_cache,
        new_keys.reshape(requests, 16, cols),
        new_values.reshape(requests, 16, cols),
    )
    return finish(
        Z,
        out.reshape(requests, Z, X, 16, cols),
        table.reshape(Z, X, 16, 128),
        wo_all,
        tokens,
    )


def solution(mesh):
    placed = (
        P(None, "seq", None),
        P(None, "seq", None),
        P(None, "seq"),
        P(),
        P(),
        P(),
        P("seq", "head"),
        P("seq", "head"),
        P("seq", "head"),
        P("seq", "head"),
        P("seq", None, "head"),
        P("seq", None, "head"),
    )
    return jax.shard_map(
        functools.partial(per_device, mesh.shape["seq"] // X),
        mesh=mesh,
        in_specs=placed,
        out_specs=(P(None, "seq", "head"), P(None, "seq", "head")),
        check_vma=False,
    )
```

```python
import functools

import jax
import jax.numpy as jnp
from jax import lax
from jax.experimental import pallas as pl
from jax.experimental.pallas import tpu as pltpu
from jax.sharding import PartitionSpec as P

HD = 128
PAGE = 128
MAXP = 64
X = 4
BLK = 160
COVER = 256
MESH = pl.DeviceIdType.MESH
F32 = jnp.float32
BF16 = jnp.bfloat16
NT = (((1,), (1,)), ((), ()))
TN = (((0,), (0,)), ((), ()))


def in_hbm(*arrays):
    return [pltpu.with_memory_space_constraint(array, pltpu.HBM) for array in arrays]


def place(Z):
    seq = lax.axis_index("seq")
    head = lax.axis_index("head")
    z, x = seq // X, lax.rem(seq, X)

    def at(dz, dx):
        return (lax.rem(z + dz + Z, Z) * X + lax.rem(x + dx, X), head)

    return seq, head, z, x, at


def greet(partners):
    barrier = pltpu.get_barrier_semaphore()
    for partner in partners:
        pl.semaphore_signal(barrier, inc=1, device_id=partner, device_id_type=MESH)
    pl.semaphore_wait(barrier, len(partners))


def remote(src, dst, send, recv, target):
    return pltpu.make_async_remote_copy(
        src_ref=src, dst_ref=dst, send_sem=send, recv_sem=recv, device_id=target, device_id_type=MESH
    )


def project_kernel(
    Z,
    x_hbm,
    a_hbm,
    mask_hbm,
    gain_hbm,
    cos_ref,
    sin_ref,
    wq_ref,
    wk_ref,
    wv_ref,
    q_all,
    kn_ref,
    vn_ref,
    xs,
    as_,
    mask_ref,
    gain,
    xn,
    xg,
    wb,
    acc,
    part,
    got,
    qloc,
    ring_send,
    ring_recv,
    tok_send,
    tok_recv,
    core_send,
    core_recv,
    part_send,
    part_recv,
    zq_send,
    zq_recv,
    xq_send,
    xq_recv,
    local_sem,
):
    seq, head, z, x, at = place(Z)
    width = X * BLK
    off = pl.multiple_of(32 * x, 32)
    own = (wq_ref, wk_ref, wv_ref)
    half = xs.shape[0]
    core = lax.rem(head, 2)
    partner = (seq, head + 1 - 2 * core)
    ours = pl.ds(core * half, half)
    loads = [
        pltpu.make_async_copy(x_hbm.at[ours], xs, local_sem.at[0]),
        pltpu.make_async_copy(a_hbm.at[ours], as_, local_sem.at[1]),
        pltpu.make_async_copy(gain_hbm, gain, local_sem.at[2]),
        pltpu.make_async_copy(mask_hbm, mask_ref, local_sem.at[8]),
    ]
    for copy in loads:
        copy.start()
    kept = [pltpu.make_async_copy(own[t], wb.at[t, z, pl.ds(off, BLK)], local_sem.at[3 + t]) for t in range(3)]
    for copy in kept:
        copy.start()
    greet([at(d, 0) for d in range(1, Z)] + [at(0, d) for d in range(1, X)] + [partner])

    def ring(right, t, k):
        block = lax.rem(z - k + Z, Z) if right else lax.rem(z + k, Z)
        slot = wb.at[t, block, pl.ds(off, BLK)]
        src = own[t] if k == 0 else slot
        way = 1 if right else 0
        return remote(
            src, slot, ring_send.at[way, t, k], ring_recv.at[way, t, k], at(1 if right else -1, 0)
        )

    def steps(t, right):
        return Z // 2 if right == (t % 2 == 0) else Z - 1 - Z // 2

    def advance(tensors, k):
        for t in tensors:
            for right in (True, False):
                if 0 < k <= steps(t, right):
                    ring(right, t, k - 1).wait_recv()
                if k < steps(t, right):
                    ring(right, t, k).start()

    advance((0, 1), 0)
    for copy in loads:
        copy.wait()

    diagonal = lax.broadcasted_iota(jnp.int32, (8, 8), 0) == lax.broadcasted_iota(jnp.int32, (8, 8), 1)

    @pl.loop(0, half)
    def _(r):
        accept = mask_ref[pl.ds(core * half + r, 1), :].astype(F32)
        accept = jnp.sum(jnp.where(diagonal, accept, 0.0), axis=1, keepdims=True)
        first = xs[r].astype(F32)
        second = jnp.where(accept == 1.0, as_[r].astype(F32), first)
        both = jnp.concatenate([first, second], axis=0)
        inverse = lax.rsqrt(jnp.mean(both * both, axis=-1, keepdims=True) + 1e-05)
        normed = (both * inverse * gain[...]).astype(BF16)
        rows = pl.ds(pl.multiple_of(r * 16, 16), 16)
        for c in range(Z):
            xn[c, rows, :] = normed[:, c * width : (c + 1) * width]

    share = half * 16
    mine = pl.ds(pl.multiple_of(x * 128, 128), 128)

    def cover(there):
        return xn.at[:, :, pl.ds(pl.multiple_of(there * 128, 128), COVER)]

    def rows_of(source):
        return xg.at[:, pl.ds(pl.multiple_of(source * 128 + core * share, share), share)]

    def token(d):
        return remote(cover(lax.rem(x + d, X)), rows_of(x), tok_send.at[d - 1], tok_recv.at[d - 1], at(0, d))

    def across(d):
        slot = rows_of(lax.rem(x - d + X, X))
        return remote(cover(x) if d == 0 else slot, slot, core_send.at[d], core_recv.at[d], partner)

    for d in (2, 1, 3):
        token(d).start()
    across(0).start()
    own_tokens = pltpu.make_async_copy(cover(x), rows_of(x), local_sem.at[6])
    own_tokens.start()

    zero = jnp.zeros((32, wb.shape[3]), BF16)

    @pl.loop(0, Z)
    def _(c):
        for t in range(3):
            for j in range(3):
                stripe = pl.multiple_of(32 * lax.rem(x + 5 + j, 8), 32)
                wb[t, c, pl.ds(stripe, 32), :] = zero

    acc[...] = jnp.zeros_like(acc)
    advance((0, 1), 1)
    advance((0, 1), 2)
    for d in (1, 3, 2):
        token(d).wait_recv()
        across(d).start()
    advance((0, 1), 3)
    advance((2,), 0)
    own_tokens.wait()
    for copy in kept:
        copy.wait()
    for d in range(X):
        across(d).wait_recv()

    def multiply(t, low, high):
        @pl.loop(low, high)
        def _(j):
            block = lax.rem(z + (1 - 2 * lax.rem(j, 2)) * ((j + 1) // 2) + Z, Z)
            acc[t] += jnp.dot(xg[block], wb[t, block], preferred_element_type=F32)

    def piece(t, d):
        return remote(
            part.at[t, d - 1], got.at[t, d - 1], part_send.at[t, d - 1], part_recv.at[t, d - 1], at(0, d)
        )

    def spread(t):
        for d in (2, 1, 3):
            there = lax.rem(x + d, X)
            part[t, d - 1] = acc[t, pl.ds(pl.multiple_of(there * 128, 128), 128), :].astype(BF16)
            piece(t, d).start()

    def collect(t):
        total = acc[t, mine, :]
        for d in range(1, X):
            piece(t, d).wait_recv()
            total = total + got[t, d - 1].astype(F32)
        return total

    def turn(rows):
        pieces = []
        for h in range(rows.shape[1] // HD):
            piece = rows[:, h * HD : (h + 1) * HD]
            pieces.append(piece * cos_ref[...] + pltpu.roll(piece, HD // 2, 1) * sin_ref[...])
        return jnp.concatenate(pieces, axis=1).astype(BF16)

    multiply(0, 0, Z - 1)
    multiply(1, 0, Z - 1)
    advance((0, 1), 4)
    multiply(0, Z - 1, Z)
    spread(0)
    multiply(1, Z - 1, Z)
    spread(1)
    advance((2,), 1)
    query = turn(collect(0))
    for r in range(qloc.shape[0]):
        qloc[r] = query[r * 16 : (r + 1) * 16]
    own_query = pltpu.make_async_copy(qloc, q_all.at[:, seq], local_sem.at[7])
    own_query.start()

    def to_z(right, k):
        slot = q_all.at[:, (lax.rem(z - k + Z, Z) if right else lax.rem(z + k, Z)) * X + x]
        i = 1 if right else 0
        return remote(
            qloc if k == 0 else slot, slot, zq_send.at[i, k], zq_recv.at[i, k], at(1 if right else -1, 0)
        )

    hops = {True: Z // 2, False: Z - 1 - Z // 2}

    def to_x(dz, way):
        slot = q_all.at[:, lax.rem(z - dz + Z, Z) * X + x]
        i = (way + 1) // 2
        return remote(qloc if dz == 0 else slot, slot, xq_send.at[i, 0, dz], xq_recv.at[i, 0, dz], at(0, way + X))

    def onward(dz):
        way = 1 - 2 * (dz % 2)
        slot = q_all.at[:, lax.rem(z - dz + Z, Z) * X + lax.rem(x - way + X, X)]
        i = (way + 1) // 2
        return remote(slot, slot, xq_send.at[i, 1, dz], xq_recv.at[i, 1, dz], at(0, way + X))

    arrival = [0] + sorted(range(1, Z), key=lambda d: min(d, Z - d))

    def pass_on(low, high):
        for i in range(low, high):
            if i < Z:
                dz = arrival[i]
                if dz:
                    right = dz <= hops[True]
                    k = dz if right else Z - dz
                    to_z(right, k - 1).wait_recv()
                    if k < hops[right]:
                        to_z(right, k).start()
                to_x(dz, 1).start()
                to_x(dz, -1).start()
            if i > 0:
                dz = arrival[i - 1]
                to_x(dz, 1 - 2 * (dz % 2)).wait_recv()
                onward(dz).start()

    to_z(True, 0).start()
    to_z(False, 0).start()
    pass_on(0, 1)
    advance((2,), 2)
    kn_ref[...] = turn(collect(1))
    advance((2,), 3)
    pass_on(1, 3)
    advance((2,), 4)
    multiply(2, 0, Z)
    spread(2)
    pass_on(3, Z + 1)
    vn_ref[...] = collect(2).astype(BF16)

    own_query.wait()
    for t in range(3):
        for right in (True, False):
            for k in range(steps(t, right)):
                ring(right, t, k).wait_send()
        for d in range(1, X):
            piece(t, d).wait_send()
    for d in range(1, X):
        token(d).wait_send()
    for d in range(X):
        across(d).wait_send()
    for right in (True, False):
        for k in range(hops[right]):
            to_z(right, k).wait_send()
    for dz in range(Z):
        forwarded = 1 - 2 * (dz % 2)
        to_x(dz, -forwarded).wait_recv()
        onward(dz).wait()
        to_x(dz, 1).wait_send()
        to_x(dz, -1).wait_send()


def project(Z, block_input, accepted, mask, gain, cosine, sine, w_query, w_key, w_value):
    requests, tokens, width = block_input.shape
    cols = w_query.shape[1]
    rows = requests * 16
    vmem = pl.BlockSpec(memory_space=pltpu.VMEM)
    hbm = pl.BlockSpec(memory_space=pltpu.HBM)
    dma = pltpu.SemaphoreType.DMA
    return pl.pallas_call(
        functools.partial(project_kernel, Z),
        name="project",
        out_shape=(
            jax.ShapeDtypeStruct((requests, Z * X, 16, cols), BF16),
            jax.ShapeDtypeStruct((rows, cols), BF16),
            jax.ShapeDtypeStruct((rows, cols), BF16),
        ),
        in_specs=[hbm, hbm, hbm, hbm, vmem, vmem, hbm, hbm, hbm],
        out_specs=(vmem, vmem, vmem),
        scratch_shapes=[
            pltpu.VMEM((requests // 2, tokens, width), BF16),
            pltpu.VMEM((requests // 2, tokens, width), BF16),
            pltpu.VMEM(mask.shape, jnp.int32),
            pltpu.VMEM((1, width), F32),
            pltpu.VMEM((Z, rows // 2, X * BLK), BF16),
            pltpu.VMEM((Z, X * rows, COVER), BF16),
            pltpu.VMEM((3, Z, COVER, cols), BF16),
            pltpu.VMEM((3, X * rows, cols), F32),
            pltpu.VMEM((3, X - 1, rows, cols), BF16),
            pltpu.VMEM((3, X - 1, rows, cols), BF16),
            pltpu.VMEM((requests, 16, cols), BF16),
            dma((2, 3, Z // 2)),
            dma((2, 3, Z // 2)),
            dma((X - 1,)),
            dma((X - 1,)),
            dma((X,)),
            dma((X,)),
            dma((3, X - 1)),
            dma((3, X - 1)),
            dma((2, Z // 2)),
            dma((2, Z // 2)),
            dma((2, 2, Z)),
            dma((2, 2, Z)),
            dma((9,)),
        ],
        compiler_params=pltpu.CompilerParams(
            collective_id=0, has_side_effects=True, vmem_limit_bytes=24 << 20
        ),
    )(*in_hbm(block_input, accepted, mask, gain), cosine, sine, *in_hbm(w_query, w_key, w_value))


def attend_kernel(
    base,
    lengths_hbm,
    table_hbm,
    q_ref,
    k_ref,
    v_hbm,
    kn_ref,
    vn_ref,
    o_ref,
    st_ref,
    acc,
    stats,
    qt,
    v_ref,
    table_ref,
    lengths,
    owner,
    live,
    sems,
):
    heads = acc.shape[1]
    queries = acc.shape[3]
    scale = HD ** (-0.5)
    loads = [
        pltpu.make_async_copy(lengths_hbm, lengths, sems.at[0]),
        pltpu.make_async_copy(table_hbm, table_ref, sems.at[1]),
        pltpu.make_async_copy(v_hbm, v_ref, sems.at[2]),
    ]
    for copy in loads:
        copy.start()
    stats[...] = jnp.zeros_like(stats)

    key_pass = lax.broadcasted_iota(jnp.int32, (16, queries), 0) // 8
    query_pass = lax.rem(lax.broadcasted_iota(jnp.int32, (16, queries), 1) // 8, 2)
    same = key_pass == query_pass

    @pl.loop(0, q_ref.shape[0])
    def _(r):
        for h in range(heads):
            col = slice(h * HD, (h + 1) * HD)
            qt[r, h] = jnp.transpose(q_ref[r, :, col])
            scores = jnp.dot(kn_ref[r, :, col], qt[r, h], preferred_element_type=F32) * scale
            scores = jnp.where(same, scores, -1e30)
            peak = jnp.max(scores, axis=0, keepdims=True)
            weights = jnp.where(same, jnp.exp(scores - peak), 0.0)
            high = weights.astype(BF16)
            low = (weights - high.astype(F32)).astype(BF16)
            values = vn_ref[r, :, col]
            acc[r, h] = lax.dot_general(
                jnp.concatenate([values, values], axis=0),
                jnp.concatenate([high, low], axis=0),
                TN,
                preferred_element_type=F32,
            )
            stats[pl.ds(r * 8 + h, 1), :] = peak
            stats[pl.ds(r * 8 + 4 + h, 1), :] = jnp.sum(weights, axis=0, keepdims=True)

    for copy in loads:
        copy.wait()
    shape = table_ref.shape
    slots = lax.broadcasted_iota(jnp.int32, shape, 0) * shape[1] + lax.broadcasted_iota(jnp.int32, shape, 1)
    slots = slots.astype(F32)
    for p in range(k_ref.shape[0]):
        found = jnp.sum(jnp.where(table_ref[...] == base[0] + p, slots, 0.0)).astype(jnp.int32)
        owner[p] = found // MAXP
        live[p] = lengths[found // MAXP] - lax.rem(found, MAXP) * PAGE

    slot = lax.broadcasted_iota(jnp.int32, (PAGE, queries), 0)

    @pl.loop(0, k_ref.shape[0])
    def _(p):
        r = owner[p]

        @pl.when(live[p] > 0)
        def _():
            alive = slot < live[p]
            for h in range(heads):
                col = slice(h * HD, (h + 1) * HD)
                scores = jnp.dot(k_ref[p, :, col], qt[r, h], preferred_element_type=F32) * scale
                scores = jnp.where(alive, scores, -1e30)
                page_peak = jnp.max(scores, axis=0, keepdims=True)
                weights = jnp.exp(scores - page_peak)
                page_out = lax.dot_general(
                    v_ref[p, :, col], weights.astype(BF16), TN, preferred_element_type=F32
                )
                m_row = pl.ds(r * 8 + h, 1)
                l_row = pl.ds(r * 8 + 4 + h, 1)
                before = stats[m_row, :]
                after = jnp.maximum(before, page_peak)
                old, new = jnp.exp(before - after), jnp.exp(page_peak - after)
                acc[r, h] = acc[r, h] * old + page_out * new
                stats[m_row, :] = after
                stats[l_row, :] = stats[l_row, :] * old + jnp.sum(weights, axis=0, keepdims=True) * new

    @pl.loop(0, q_ref.shape[0])
    def _(r):
        for h in range(heads):
            o_ref[r, :, h * HD : (h + 1) * HD] = jnp.transpose(acc[r, h].astype(BF16))

    st_ref[...] = jnp.transpose(stats[...])


def attend(base, lengths, page_table, q_all, key_cache, value_cache, new_keys, new_values):
    requests, queries, cols = q_all.shape
    pages = key_cache.shape[0]
    heads = cols // HD
    vmem = pl.BlockSpec(memory_space=pltpu.VMEM)
    smem = pl.BlockSpec(memory_space=pltpu.SMEM)
    hbm = pl.BlockSpec(memory_space=pltpu.HBM)
    return pl.pallas_call(
        attend_kernel,
        name="attend",
        out_shape=(
            jax.ShapeDtypeStruct((requests, queries, cols), BF16),
            jax.ShapeDtypeStruct((queries, 128), F32),
        ),
        in_specs=[smem, hbm, hbm, vmem, vmem, hbm, vmem, vmem],
        out_specs=(vmem, vmem),
        scratch_shapes=[
            pltpu.VMEM((requests, heads, HD, queries), F32),
            pltpu.VMEM((128, queries), F32),
            pltpu.VMEM((requests, heads, HD, queries), BF16),
            pltpu.VMEM(value_cache.shape, BF16),
            pltpu.VMEM(page_table.shape, jnp.int32),
            pltpu.SMEM(lengths.shape, jnp.int32),
            pltpu.SMEM((pages,), jnp.int32),
            pltpu.SMEM((pages,), jnp.int32),
            pltpu.SemaphoreType.DMA((3,)),
        ],
        compiler_params=pltpu.CompilerParams(vmem_limit_bytes=20 << 20),
    )(base, *in_hbm(lengths, page_table), q_all, key_cache, *in_hbm(value_cache), new_keys, new_values)


def join(tables):
    peak = functools.reduce(jnp.maximum, tables)
    factors = [jnp.exp(table - peak) for table in tables]
    total = sum(pltpu.roll(factor, 4, 1) * table for factor, table in zip(factors, tables))
    lane = lax.broadcasted_iota(jnp.int32, peak.shape, 1)
    return jnp.where(lax.rem(lane, 8) >= 4, total, peak), factors


def weigh(factors, sources, r, h):
    lane = r * 8 + h
    return sum(
        factor[:, lane : lane + 1] * source[:, h * HD : (h + 1) * HD].astype(F32)
        for factor, source in zip(factors, sources)
    )


def finish_kernel(
    Z,
    o_ref,
    st_ref,
    wo_ref,
    first_ref,
    second_ref,
    far,
    far_st,
    near,
    near_st,
    pair,
    pair_st,
    both,
    both_st,
    cb,
    cb_st,
    rb,
    rb_st,
    wo_all,
    ctx,
    pb,
    pc,
    mm,
    pm,
    ph,
    ob,
    of,
    ring_send,
    ring_recv,
    x_send,
    x_recv,
    xs_send,
    xs_recv,
    b_send,
    b_recv,
    bs_send,
    bs_recv,
    c_send,
    c_recv,
    d_send,
    d_recv,
    y_send,
    y_recv,
    e_send,
    e_recv,
    local_sem,
):
    seq, head, z, x, at = place(Z)
    requests = o_ref.shape[0]
    heads = o_ref.shape[4] // HD
    ys = Z // 2
    core, y = lax.rem(head, 2), head // 2
    partner = (seq, head + 1 - 2 * core)

    def along_y(d):
        return (seq, lax.rem(y + d, ys) * 2 + core)

    kept = pltpu.make_async_copy(wo_ref, wo_all.at[z // 2, lax.rem(z, 2)], local_sem.at[0])
    kept.start()
    greet(
        [at(d, 0) for d in range(1, Z)]
        + [at(0, d) for d in range(1, X)]
        + [along_y(d) for d in range(1, ys)]
        + [partner]
    )

    def far_off(i):
        return Z // 2 + (1 - 2 * lax.rem(i, 2)) * ((i + 1) // 2)

    def chunk(i):
        return lax.rem(z + far_off(i), Z), 1 - 2 * lax.rem(i, 2)

    def step_x(n):
        return lax.rem(x + n + X, X)

    def send_far(i):
        there, way = chunk(i)
        return (
            remote(o_ref.at[:, there, step_x(2)], far.at[there], x_send.at[0, i], x_recv.at[0, i], at(0, way + X)),
            remote(st_ref.at[there, step_x(2)], far_st.at[there], xs_send.at[0, i], xs_recv.at[0, i], at(0, way + X)),
        )

    def send_near(i):
        there, way = chunk(i)
        to = step_x(-way)
        return (
            remote(o_ref.at[:, there, to], near.at[there], x_send.at[1, i], x_recv.at[1, i], at(0, X - way)),
            remote(st_ref.at[there, to], near_st.at[there], xs_send.at[1, i], xs_recv.at[1, i], at(0, X - way)),
        )

    def send_pair(i):
        there, way = chunk(i)
        return (
            remote(pair.at[there], both.at[there], x_send.at[2, i], x_recv.at[2, i], at(0, way + X)),
            remote(pair_st.at[there], both_st.at[there], xs_send.at[2, i], xs_recv.at[2, i], at(0, way + X)),
        )

    def send_z(i):
        there, _ = chunk(i)
        target = (there * X + x, head)
        return (
            remote(cb.at[there], rb.at[i], b_send.at[i], b_recv.at[i], target),
            remote(cb_st.at[there], rb_st.at[i], bs_send.at[i], bs_recv.at[i], target),
        )

    def ring(right, k, src=None):
        block = lax.rem(z - k + Z, Z) if right else lax.rem(z + k, Z)
        way = 1 if right else 0
        slot = wo_all.at[block // 2, lax.rem(block, 2)]
        return remote(
            slot if src is None else src,
            slot,
            ring_send.at[way, k],
            ring_recv.at[way, k],
            at(1 if right else -1, 0),
        )

    right_steps, left_steps = Z // 2, Z - 1 - Z // 2

    def begin(i):
        for copy in send_far(i) + send_near(i):
            copy.start()

    begin(0)
    begin(1)
    begin(2)
    ring(True, 0, wo_ref).start()
    ring(False, 0, wo_ref).start()
    kept.wait()

    def middle(i):
        there, way = chunk(i)
        for copy in send_far(i):
            copy.wait_recv()
        table, factors = join([st_ref[there, step_x(way)], far_st[there]])
        pair_st[there] = table
        for r in range(requests):
            for h in range(heads):
                value = weigh(factors, [o_ref[r, there, step_x(way)], far[there, r]], r, h)
                pair[there, r, :, h * HD : (h + 1) * HD] = value.astype(BF16)
        for copy in send_pair(i):
            copy.start()

    def end(i):
        there, _ = chunk(i)
        for copy in send_near(i) + send_pair(i):
            copy.wait_recv()
        table, factors = join([st_ref[there, x], near_st[there], both_st[there]])
        cb_st[there] = table
        for r in range(requests):
            for h in range(heads):
                value = weigh(factors, [o_ref[r, there, x], near[there, r], both[there, r]], r, h)
                cb[there, r, :, h * HD : (h + 1) * HD] = value.astype(BF16)

    middle(0)

    @pl.loop(1, Z)
    def _(i):
        @pl.when(i + 2 < Z)
        def _():
            begin(i + 2)

        middle(i)
        end(i - 1)
        for copy in send_z(i - 1):
            copy.start()

        @pl.when(i < right_steps)
        def _():
            ring(True, i - 1).wait_recv()
            ring(True, i).start()

        @pl.when(i < left_steps)
        def _():
            ring(False, i - 1).wait_recv()
            ring(False, i).start()

    end(Z - 1)
    for i in range(Z - 1):
        for copy in send_z(i):
            copy.wait_recv()

    mine = pl.multiple_of(x * 128, 128)
    table, factors = join([cb_st[z]] + [rb_st[i] for i in range(Z - 1)])
    inverse = 1.0 / table

    def share(half, d):
        rows = ctx.at[pl.ds(pl.multiple_of(mine + half * 64, 64), 64)]
        return remote(rows, rows, c_send.at[half, d - 1], c_recv.at[half, d - 1], at(0, d))

    for r in range(requests):
        sources = [cb[z, r]] + [rb[i, r] for i in range(Z - 1)]
        for h in range(heads):
            lane = r * 8 + h + 4
            value = weigh(factors, sources, r, h) * inverse[:, lane : lane + 1]
            ctx[pl.ds(mine + r * 16, 16), h * HD : (h + 1) * HD] = value.astype(BF16)
        if r % 4 == 3:
            for d in (2, 1, 3):
                share(r // 4, d).start()

    shares = [share(half, d) for half in range(2) for d in range(1, X)]
    ring(True, right_steps - 1).wait_recv()
    ring(False, left_steps - 1).wait_recv()
    for copy in shares:
        copy.wait_recv()

    def multiply(c):
        weights = wo_all[:, c].reshape(ys * BLK, ctx.shape[1])
        result = lax.dot_general(weights, ctx[...], NT, preferred_element_type=F32)
        return result.reshape(ys, BLK, ctx.shape[0])

    def to_core(d):
        there = lax.rem(y + d, ys)
        return remote(pb.at[there], pc.at[there], d_send.at[d], d_recv.at[d], partner)

    def to_y(d):
        return remote(pm.at[d - 1], ph.at[d - 1], y_send.at[d - 1], y_recv.at[d - 1], along_y(d))

    pb[...] = multiply(1 - core).astype(BF16)
    for d in (2, 1, 3, 0):
        to_core(d).start()
    mm[...] = multiply(core)
    for d in (2, 1, 3):
        there = lax.rem(y + d, ys)
        to_core(d).wait_recv()
        pm[d - 1] = (mm[there] + pc[there].astype(F32)).astype(BF16)
        to_y(d).start()

    to_core(0).wait_recv()
    total = mm[y] + pc[y].astype(F32)
    for d in range(1, ys):
        to_y(d).wait_recv()
        total = total + ph[d - 1].astype(F32)
    ob[...] = total.astype(BF16)
    block = pl.ds(pl.multiple_of(x * BLK, 32), BLK)

    def to_owner(d):
        there = pl.multiple_of(lax.rem(x + d, X) * 128, 128)
        return remote(ob.at[:, pl.ds(there, 128)], of.at[block], e_send.at[d - 1], e_recv.at[d - 1], at(0, d))

    for d in (2, 1, 3):
        to_owner(d).start()
    last = pltpu.make_async_copy(ob.at[:, pl.ds(mine, 128)], of.at[block], local_sem.at[1])
    last.start()
    last.wait()
    for d in range(1, X):
        to_owner(d).wait_recv()
    result = jnp.transpose(of[...].astype(F32))
    for r in range(requests):
        first_ref[r] = result[r * 16 : r * 16 + 8].astype(BF16)
        second_ref[r] = result[r * 16 + 8 : r * 16 + 16].astype(BF16)

    @pl.loop(0, Z)
    def _(i):
        for copy in send_far(i) + send_near(i) + send_pair(i):
            copy.wait_send()

    for k in range(right_steps):
        ring(True, k).wait_send()
    for k in range(left_steps):
        ring(False, k).wait_send()
    for i in range(Z - 1):
        for copy in send_z(i):
            copy.wait_send()
    for copy in shares:
        copy.wait_send()
    for d in range(1, X):
        to_owner(d).wait_send()
    for d in range(ys):
        to_core(d).wait_send()
    for d in range(1, ys):
        to_y(d).wait_send()


def finish(Z, out, table, w_out, tokens):
    requests = out.shape[0]
    cols = out.shape[4]
    rows = requests * 16
    ys = Z // 2
    vmem = pl.BlockSpec(memory_space=pltpu.VMEM)
    hbm = pl.BlockSpec(memory_space=pltpu.HBM)
    dma = pltpu.SemaphoreType.DMA
    shape = jax.ShapeDtypeStruct((requests, tokens, X * BLK), BF16)
    chunks = pltpu.VMEM((Z, requests, 16, cols), BF16)
    tables = pltpu.VMEM((Z, 16, 128), F32)
    return pl.pallas_call(
        functools.partial(finish_kernel, Z),
        name="finish",
        out_shape=(shape, shape),
        in_specs=[vmem, vmem, hbm],
        out_specs=(vmem, vmem),
        scratch_shapes=[
            chunks,
            tables,
            chunks,
            tables,
            chunks,
            tables,
            chunks,
            tables,
            chunks,
            tables,
            pltpu.VMEM((Z - 1, requests, 16, cols), BF16),
            pltpu.VMEM((Z - 1, 16, 128), F32),
            pltpu.VMEM((ys, 2, BLK, cols), BF16),
            pltpu.VMEM((X * rows, cols), BF16),
            pltpu.VMEM((ys, BLK, X * rows), BF16),
            pltpu.VMEM((ys, BLK, X * rows), BF16),
            pltpu.VMEM((ys, BLK, X * rows), F32),
            pltpu.VMEM((ys - 1, BLK, X * rows), BF16),
            pltpu.VMEM((ys - 1, BLK, X * rows), BF16),
            pltpu.VMEM((BLK, X * rows), BF16),
            pltpu.VMEM((X * BLK, rows), BF16),
            dma((2, Z // 2)),
            dma((2, Z // 2)),
            dma((3, Z)),
            dma((3, Z)),
            dma((3, Z)),
            dma((3, Z)),
            dma((Z - 1,)),
            dma((Z - 1,)),
            dma((Z - 1,)),
            dma((Z - 1,)),
            dma((2, X - 1)),
            dma((2, X - 1)),
            dma((ys,)),
            dma((ys,)),
            dma((ys - 1,)),
            dma((ys - 1,)),
            dma((X - 1,)),
            dma((X - 1,)),
            dma((2,)),
        ],
        compiler_params=pltpu.CompilerParams(
            collective_id=1, has_side_effects=True, vmem_limit_bytes=20 << 20
        ),
    )(out, table, *in_hbm(w_out))


def per_device(
    Z,
    block_input,
    accepted,
    accept_mask,
    cache_lengths,
    page_table,
    norm_gain,
    w_query,
    w_key,
    w_value,
    w_out,
    key_cache,
    value_cache,
):
    seq = lax.axis_index("seq")
    requests, tokens, width = block_input.shape
    half = HD // 2
    frequency = 10000.0 ** (-(jnp.arange(half).astype(F32) * 2.0) / HD)
    positions = (
        cache_lengths[:, None] + seq * tokens + jnp.arange(tokens, dtype=jnp.int32)[None, :]
    ).astype(F32)
    angles = jnp.broadcast_to(positions[:, None, :, None] * frequency, (requests, 2, tokens, half))
    angles = angles.reshape(requests * 2 * tokens, half)
    cosine, sine = jnp.cos(angles), jnp.sin(angles)
    cosine = jnp.concatenate([cosine, cosine], axis=1)
    sine = jnp.concatenate([-sine, sine], axis=1)

    q_all, new_keys, new_values = project(
        Z,
        block_input,
        accepted,
        accept_mask,
        norm_gain.reshape(1, width),
        cosine,
        sine,
        w_query,
        w_key,
        w_value,
    )
    cols = q_all.shape[3]
    queries = Z * X * 16
    out, table = attend(
        (seq * key_cache.shape[0]).astype(jnp.int32).reshape(1),
        cache_lengths,
        page_table.reshape(-1, 128),
        q_all.reshape(requests, queries, cols),
        key_cache,
        value_cache,
        new_keys.reshape(requests, 16, cols),
        new_values.reshape(requests, 16, cols),
    )
    return finish(Z, out.reshape(requests, Z, X, 16, cols), table.reshape(Z, X, 16, 128), w_out, tokens)


def solution(mesh):
    placed = (
        P(None, "seq", None),
        P(None, "seq", None),
        P(None, "seq"),
        P(),
        P(),
        P(),
        P("seq", "head"),
        P("seq", "head"),
        P("seq", "head"),
        P("seq", "head"),
        P("seq", None, "head"),
        P("seq", None, "head"),
    )
    return jax.shard_map(
        functools.partial(per_device, mesh.shape["seq"] // X),
        mesh=mesh,
        in_specs=placed,
        out_specs=(P(None, "seq", "head"), P(None, "seq", "head")),
        check_vma=False,
    )
```

```python
import functools

import jax
import jax.numpy as jnp
from jax import lax
from jax.experimental import pallas as pl
from jax.experimental.pallas import tpu as pltpu
from jax.sharding import PartitionSpec as P

HD = 128
PAGE = 128
MAXP = 64
X = 4
BLK = 160
FIRST = 6
WINDOW = 4
LAG = 3
HOLD = 2
COVER = 256
MESH = pl.DeviceIdType.MESH
F32 = jnp.float32
BF16 = jnp.bfloat16
NT = (((1,), (1,)), ((), ()))
TN = (((0,), (0,)), ((), ()))


def in_hbm(*arrays):
    return [pltpu.with_memory_space_constraint(array, pltpu.HBM) for array in arrays]


ORDER = (
    "q1", "q2", "k0", "tf", "q3", "k1", "v0", "th", "mq07", "q4", "mq78", "sq",
    "k2", "v1", "mk05", "cq", "p0", "k3", "v2", "rx", "p1", "p2", "k4", "mk58",
    "sk", "v3", "p3", "p4", "v4", "mv08", "sv", "p5", "p6", "p7", "p8", "p9",
    "ck", "cv",
)


LATE = ("x16", "c0", "x68", "own", "wo", "m0", "c1", "m1", "y0", "y1")


def place(Z):
    seq = lax.axis_index("seq")
    head = lax.axis_index("head")
    z, x = seq // X, lax.rem(seq, X)

    def at(dz, dx):
        return (lax.rem(z + dz + Z, Z) * X + lax.rem(x + dx, X), head)

    return seq, head, z, x, at


def greet(partners):
    barrier = pltpu.get_barrier_semaphore()
    for partner in partners:
        pl.semaphore_signal(barrier, inc=1, device_id=partner, device_id_type=MESH)
    pl.semaphore_wait(barrier, len(partners))


def remote(src, dst, send, recv, target):
    return pltpu.make_async_remote_copy(
        src_ref=src, dst_ref=dst, send_sem=send, recv_sem=recv, device_id=target, device_id_type=MESH
    )


def project_kernel(
    Z,
    x_hbm,
    a_hbm,
    mask_hbm,
    gain_hbm,
    cos_ref,
    sin_ref,
    wq_ref,
    wk_ref,
    wv_ref,
    q_all,
    kn_ref,
    vn_ref,
    xs,
    as_,
    mask_ref,
    gain,
    xn,
    xg,
    wb,
    acc,
    part,
    got,
    qloc,
    ring_send,
    ring_recv,
    tok_send,
    tok_recv,
    core_send,
    core_recv,
    part_send,
    part_recv,
    zq_send,
    zq_recv,
    xq_send,
    xq_recv,
    rx_send,
    rx_recv,
    local_sem,
):
    seq, head, z, x, at = place(Z)
    width = X * BLK
    off = pl.multiple_of(32 * x, 32)
    own = (wq_ref, wk_ref, wv_ref)
    half = xs.shape[0]
    core = lax.rem(head, 2)
    partner = (seq, head + 1 - 2 * core)
    ours = pl.ds(core * half, half)
    loads = [
        pltpu.make_async_copy(x_hbm.at[ours], xs, local_sem.at[0]),
        pltpu.make_async_copy(a_hbm.at[ours], as_, local_sem.at[1]),
        pltpu.make_async_copy(gain_hbm, gain, local_sem.at[2]),
        pltpu.make_async_copy(mask_hbm, mask_ref, local_sem.at[8]),
    ]
    for copy in loads:
        copy.start()
    kept = [pltpu.make_async_copy(own[t], wb.at[t, z, pl.ds(off, BLK)], local_sem.at[3 + t]) for t in range(3)]
    for copy in kept:
        copy.start()
    greet([at(d, 0) for d in range(1, Z)] + [at(0, d) for d in range(1, X)] + [partner])

    def ring(right, t, k):
        block = lax.rem(z - k + Z, Z) if right else lax.rem(z + k, Z)
        slot = wb.at[t, block, pl.ds(off, BLK)]
        src = own[t] if k == 0 else slot
        way = 1 if right else 0
        return remote(
            src, slot, ring_send.at[way, t, k], ring_recv.at[way, t, k], at(1 if right else -1, 0)
        )

    def steps(t, right):
        return Z // 2 if right == (t % 2 == 0) else Z - 1 - Z // 2

    def advance(tensors, k):
        for t in tensors:
            for right in (True, False):
                if 0 < k <= steps(t, right):
                    ring(right, t, k - 1).wait_recv()
                if k < steps(t, right):
                    ring(right, t, k).start()

    advance((0,), 0)
    for copy in loads:
        copy.wait()

    diagonal = lax.broadcasted_iota(jnp.int32, (8, 8), 0) == lax.broadcasted_iota(jnp.int32, (8, 8), 1)

    @pl.loop(0, half)
    def _(r):
        accept = mask_ref[pl.ds(core * half + r, 1), :].astype(F32)
        accept = jnp.sum(jnp.where(diagonal, accept, 0.0), axis=1, keepdims=True)
        first = xs[r].astype(F32)
        second = jnp.where(accept == 1.0, as_[r].astype(F32), first)
        both = jnp.concatenate([first, second], axis=0)
        inverse = lax.rsqrt(jnp.mean(both * both, axis=-1, keepdims=True) + 1e-05)
        normed = (both * inverse * gain[...]).astype(BF16)
        rows = pl.ds(pl.multiple_of(r * 16, 16), 16)
        for c in range(Z):
            xn[c, rows, :] = normed[:, c * width : (c + 1) * width]

    share = half * 16
    mine = pl.ds(pl.multiple_of(x * 128, 128), 128)

    def cover(there):
        return xn.at[:, :, pl.ds(pl.multiple_of(there * 128, 128), COVER)]

    def rows_of(source):
        return xg.at[:, pl.ds(pl.multiple_of(source * 128 + core * share, share), share)]

    def token(d):
        return remote(cover(lax.rem(x + d, X)), rows_of(x), tok_send.at[d - 1], tok_recv.at[d - 1], at(0, d))

    def across(d):
        slot = rows_of(lax.rem(x - d + X, X))
        return remote(cover(x) if d == 0 else slot, slot, core_send.at[d], core_recv.at[d], partner)

    for d in (2, 1, 3):
        token(d).start()
    across(0).start()
    own_tokens = pltpu.make_async_copy(cover(x), rows_of(x), local_sem.at[6])
    own_tokens.start()

    zero = jnp.zeros((32, wb.shape[3]), BF16)

    @pl.loop(0, Z)
    def _(c):
        for t in range(3):
            for j in range(3):
                stripe = pl.multiple_of(32 * lax.rem(x + 5 + j, 8), 32)
                wb[t, c, pl.ds(stripe, 32), :] = zero

    acc[...] = jnp.zeros_like(acc)
    def multiply(t, low, high):
        @pl.loop(low, high)
        def _(j):
            block = lax.rem(z + (1 - 2 * lax.rem(j, 2)) * ((j + 1) // 2) + Z, Z)
            acc[t] += jnp.dot(xg[block], wb[t, block], preferred_element_type=F32)

    def piece(t, d):
        return remote(
            part.at[t, d - 1], got.at[t, d - 1], part_send.at[t, d - 1], part_recv.at[t, d - 1], at(0, d)
        )

    def spread(t):
        for d in (2, 1, 3):
            there = lax.rem(x + d, X)
            part[t, d - 1] = acc[t, pl.ds(pl.multiple_of(there * 128, 128), 128), :].astype(BF16)
            piece(t, d).start()

    def collect(t):
        total = acc[t, mine, :]
        for d in range(1, X):
            piece(t, d).wait_recv()
            total = total + got[t, d - 1].astype(F32)
        return total

    def turn(rows):
        pieces = []
        for h in range(rows.shape[1] // HD):
            piece = rows[:, h * HD : (h + 1) * HD]
            pieces.append(piece * cos_ref[...] + pltpu.roll(piece, HD // 2, 1) * sin_ref[...])
        return jnp.concatenate(pieces, axis=1).astype(BF16)

    first = pl.ds(0, FIRST)
    rest = pl.ds(FIRST, qloc.shape[0] - FIRST)
    hops = {True: Z // 2, False: Z - 1 - Z // 2}

    def to_z(right, k):
        slot = q_all.at[first, (lax.rem(z - k + Z, Z) if right else lax.rem(z + k, Z)) * X + x]
        i = 1 if right else 0
        return remote(
            qloc.at[first] if k == 0 else slot,
            slot,
            zq_send.at[0, i, k],
            zq_recv.at[0, i, k],
            at(1 if right else -1, 0),
        )

    def to_x(dz, way):
        slot = q_all.at[first, lax.rem(z - dz + Z, Z) * X + x]
        i = (way + 1) // 2
        return remote(
            qloc.at[first] if dz == 0 else slot, slot, xq_send.at[i, 0, dz], xq_recv.at[i, 0, dz], at(0, way + X)
        )

    def onward(dz):
        way = 1 - 2 * (dz % 2)
        slot = q_all.at[first, lax.rem(z - dz + Z, Z) * X + lax.rem(x - way + X, X)]
        i = (way + 1) // 2
        return remote(slot, slot, xq_send.at[i, 1, dz], xq_recv.at[i, 1, dz], at(0, way + X))

    def rest_x(d):
        return remote(qloc.at[rest], q_all.at[rest, seq], rx_send.at[d - 1], rx_recv.at[d - 1], at(0, d))

    def rest_z(right, k):
        block = lax.rem(z - k + Z, Z) if right else lax.rem(z + k, Z)
        slot = q_all.at[rest, pl.ds(block * X, X)]
        i = 1 if right else 0
        return remote(slot, slot, zq_send.at[1, i, k], zq_recv.at[1, i, k], at(1 if right else -1, 0))

    def rest_step(right, k):
        if 0 < k <= hops[right]:
            rest_z(right, k - 1).wait_recv()
        if 0 <= k < hops[right]:
            rest_z(right, k).start()

    arrival = [0] + sorted(range(1, Z), key=lambda d: min(d, Z - d))

    def pass_on(low, high):
        for i in range(low, high):
            if i < Z:
                dz = arrival[i]
                if dz:
                    right = dz <= hops[True]
                    k = dz if right else Z - dz
                    to_z(right, k - 1).wait_recv()
                    if k < hops[right]:
                        to_z(right, k).start()
                    rest_step(right, k - 1)
                to_x(dz, 1).start()
                to_x(dz, -1).start()
            if i >= HOLD:
                dz = arrival[i - HOLD]
                to_x(dz, 1 - 2 * (dz % 2)).wait_recv()
                onward(dz).start()

    own_query = pltpu.make_async_copy(qloc, q_all.at[:, seq], local_sem.at[7])

    def forward_tokens():
        for d in (1, 3, 2):
            token(d).wait_recv()
            across(d).start()

    def have_tokens():
        own_tokens.wait()
        for copy in kept:
            copy.wait()
        for d in range(X):
            across(d).wait_recv()

    def query_ready():
        query = turn(collect(0))
        for r in range(qloc.shape[0]):
            qloc[r] = query[r * 16 : (r + 1) * 16]
        to_z(True, 0).start()
        to_z(False, 0).start()
        for d in (2, 1, 3):
            rest_x(d).start()
        own_query.start()

    def have_rest():
        own_query.wait()
        for d in range(1, X):
            rest_x(d).wait_recv()

    def key_ready():
        kn_ref[...] = turn(collect(1))

    def value_ready():
        vn_ref[...] = collect(2).astype(BF16)

    named = {
        "tf": forward_tokens,
        "th": have_tokens,
        "cq": query_ready,
        "rx": have_rest,
        "ck": key_ready,
        "cv": value_ready,
    }
    for word in ORDER:
        if word in named:
            named[word]()
        elif word[0] == "m":
            multiply("qkv".index(word[1]), int(word[2]), int(word[3]))
        elif word[0] == "s":
            spread("qkv".index(word[1]))
        elif word[0] == "p":
            pass_on(int(word[1]), int(word[1]) + 1)
        else:
            advance(("qkv".index(word[0]),), int(word[1]))
    rest_step(False, hops[False])
    rest_step(True, hops[True])

    for t in range(3):
        for right in (True, False):
            for k in range(steps(t, right)):
                ring(right, t, k).wait_send()
        for d in range(1, X):
            piece(t, d).wait_send()
    for d in range(1, X):
        token(d).wait_send()
    for d in range(X):
        across(d).wait_send()
    for right in (True, False):
        for k in range(hops[right]):
            to_z(right, k).wait_send()
            rest_z(right, k).wait_send()
    for d in range(1, X):
        rest_x(d).wait_send()
    for dz in range(Z):
        forwarded = 1 - 2 * (dz % 2)
        to_x(dz, -forwarded).wait_recv()
        onward(dz).wait()
        to_x(dz, 1).wait_send()
        to_x(dz, -1).wait_send()


def project(Z, block_input, accepted, mask, gain, cosine, sine, w_query, w_key, w_value):
    requests, tokens, width = block_input.shape
    cols = w_query.shape[1]
    rows = requests * 16
    vmem = pl.BlockSpec(memory_space=pltpu.VMEM)
    hbm = pl.BlockSpec(memory_space=pltpu.HBM)
    dma = pltpu.SemaphoreType.DMA
    return pl.pallas_call(
        functools.partial(project_kernel, Z),
        name="project",
        out_shape=(
            jax.ShapeDtypeStruct((requests, Z * X, 16, cols), BF16),
            jax.ShapeDtypeStruct((rows, cols), BF16),
            jax.ShapeDtypeStruct((rows, cols), BF16),
        ),
        in_specs=[hbm, hbm, hbm, hbm, vmem, vmem, hbm, hbm, hbm],
        out_specs=(vmem, vmem, vmem),
        scratch_shapes=[
            pltpu.VMEM((requests // 2, tokens, width), BF16),
            pltpu.VMEM((requests // 2, tokens, width), BF16),
            pltpu.VMEM(mask.shape, jnp.int32),
            pltpu.VMEM((1, width), F32),
            pltpu.VMEM((Z, rows // 2, X * BLK), BF16),
            pltpu.VMEM((Z, X * rows, COVER), BF16),
            pltpu.VMEM((3, Z, COVER, cols), BF16),
            pltpu.VMEM((3, X * rows, cols), F32),
            pltpu.VMEM((3, X - 1, rows, cols), BF16),
            pltpu.VMEM((3, X - 1, rows, cols), BF16),
            pltpu.VMEM((requests, 16, cols), BF16),
            dma((2, 3, Z // 2)),
            dma((2, 3, Z // 2)),
            dma((X - 1,)),
            dma((X - 1,)),
            dma((X,)),
            dma((X,)),
            dma((3, X - 1)),
            dma((3, X - 1)),
            dma((2, 2, Z // 2)),
            dma((2, 2, Z // 2)),
            dma((2, 2, Z)),
            dma((2, 2, Z)),
            dma((X - 1,)),
            dma((X - 1,)),
            dma((9,)),
        ],
        compiler_params=pltpu.CompilerParams(
            collective_id=0, has_side_effects=True, vmem_limit_bytes=24 << 20
        ),
    )(*in_hbm(block_input, accepted, mask, gain), cosine, sine, *in_hbm(w_query, w_key, w_value))


def attend_kernel(
    base,
    lengths_hbm,
    table_hbm,
    q_ref,
    k_ref,
    v_hbm,
    kn_ref,
    vn_ref,
    o_ref,
    st_ref,
    acc,
    stats,
    qt,
    v_ref,
    table_ref,
    lengths,
    owner,
    live,
    sems,
):
    heads = acc.shape[1]
    queries = acc.shape[3]
    scale = HD ** (-0.5)
    loads = [
        pltpu.make_async_copy(lengths_hbm, lengths, sems.at[0]),
        pltpu.make_async_copy(table_hbm, table_ref, sems.at[1]),
        pltpu.make_async_copy(v_hbm, v_ref, sems.at[2]),
    ]
    for copy in loads:
        copy.start()
    stats[...] = jnp.zeros_like(stats)

    key_pass = lax.broadcasted_iota(jnp.int32, (16, queries), 0) // 8
    query_pass = lax.rem(lax.broadcasted_iota(jnp.int32, (16, queries), 1) // 8, 2)
    same = key_pass == query_pass

    @pl.loop(0, q_ref.shape[0])
    def _(r):
        for h in range(heads):
            col = slice(h * HD, (h + 1) * HD)
            qt[r, h] = jnp.transpose(q_ref[r, :, col])
            scores = jnp.dot(kn_ref[r, :, col], qt[r, h], preferred_element_type=F32) * scale
            scores = jnp.where(same, scores, -1e30)
            peak = jnp.max(scores, axis=0, keepdims=True)
            weights = jnp.where(same, jnp.exp(scores - peak), 0.0)
            high = weights.astype(BF16)
            low = (weights - high.astype(F32)).astype(BF16)
            values = vn_ref[r, :, col]
            acc[r, h] = lax.dot_general(
                jnp.concatenate([values, values], axis=0),
                jnp.concatenate([high, low], axis=0),
                TN,
                preferred_element_type=F32,
            )
            stats[pl.ds(r * 8 + h, 1), :] = peak
            stats[pl.ds(r * 8 + 4 + h, 1), :] = jnp.sum(weights, axis=0, keepdims=True)

    for copy in loads:
        copy.wait()
    shape = table_ref.shape
    slots = lax.broadcasted_iota(jnp.int32, shape, 0) * shape[1] + lax.broadcasted_iota(jnp.int32, shape, 1)
    slots = slots.astype(F32)
    for p in range(k_ref.shape[0]):
        found = jnp.sum(jnp.where(table_ref[...] == base[0] + p, slots, 0.0)).astype(jnp.int32)
        owner[p] = found // MAXP
        live[p] = lengths[found // MAXP] - lax.rem(found, MAXP) * PAGE

    slot = lax.broadcasted_iota(jnp.int32, (PAGE, queries), 0)

    @pl.loop(0, k_ref.shape[0])
    def _(p):
        r = owner[p]

        @pl.when(live[p] > 0)
        def _():
            alive = slot < live[p]
            for h in range(heads):
                col = slice(h * HD, (h + 1) * HD)
                scores = jnp.dot(k_ref[p, :, col], qt[r, h], preferred_element_type=F32) * scale
                scores = jnp.where(alive, scores, -1e30)
                page_peak = jnp.max(scores, axis=0, keepdims=True)
                weights = jnp.exp(scores - page_peak)
                page_out = lax.dot_general(
                    v_ref[p, :, col], weights.astype(BF16), TN, preferred_element_type=F32
                )
                m_row = pl.ds(r * 8 + h, 1)
                l_row = pl.ds(r * 8 + 4 + h, 1)
                before = stats[m_row, :]
                after = jnp.maximum(before, page_peak)
                old, new = jnp.exp(before - after), jnp.exp(page_peak - after)
                acc[r, h] = acc[r, h] * old + page_out * new
                stats[m_row, :] = after
                stats[l_row, :] = stats[l_row, :] * old + jnp.sum(weights, axis=0, keepdims=True) * new

    @pl.loop(0, q_ref.shape[0])
    def _(r):
        for h in range(heads):
            o_ref[r, :, h * HD : (h + 1) * HD] = jnp.transpose(acc[r, h].astype(BF16))

    st_ref[...] = jnp.transpose(stats[...])


def attend(base, lengths, page_table, q_all, key_cache, value_cache, new_keys, new_values):
    requests, queries, cols = q_all.shape
    pages = key_cache.shape[0]
    heads = cols // HD
    vmem = pl.BlockSpec(memory_space=pltpu.VMEM)
    smem = pl.BlockSpec(memory_space=pltpu.SMEM)
    hbm = pl.BlockSpec(memory_space=pltpu.HBM)
    return pl.pallas_call(
        attend_kernel,
        name="attend",
        out_shape=(
            jax.ShapeDtypeStruct((requests, queries, cols), BF16),
            jax.ShapeDtypeStruct((queries, 128), F32),
        ),
        in_specs=[smem, hbm, hbm, vmem, vmem, hbm, vmem, vmem],
        out_specs=(vmem, vmem),
        scratch_shapes=[
            pltpu.VMEM((requests, heads, HD, queries), F32),
            pltpu.VMEM((128, queries), F32),
            pltpu.VMEM((requests, heads, HD, queries), BF16),
            pltpu.VMEM(value_cache.shape, BF16),
            pltpu.VMEM(page_table.shape, jnp.int32),
            pltpu.SMEM(lengths.shape, jnp.int32),
            pltpu.SMEM((pages,), jnp.int32),
            pltpu.SMEM((pages,), jnp.int32),
            pltpu.SemaphoreType.DMA((3,)),
        ],
        compiler_params=pltpu.CompilerParams(vmem_limit_bytes=20 << 20),
    )(base, *in_hbm(lengths, page_table), q_all, key_cache, *in_hbm(value_cache), new_keys, new_values)


def join(tables):
    peak = functools.reduce(jnp.maximum, tables)
    factors = [jnp.exp(table - peak) for table in tables]
    total = sum(pltpu.roll(factor, 4, 1) * table for factor, table in zip(factors, tables))
    lane = lax.broadcasted_iota(jnp.int32, peak.shape, 1)
    return jnp.where(lax.rem(lane, 8) >= 4, total, peak), factors


def weigh(factors, sources, r, h):
    lane = r * 8 + h
    return sum(
        factor[:, lane : lane + 1] * source[:, h * HD : (h + 1) * HD].astype(F32)
        for factor, source in zip(factors, sources)
    )


def finish_kernel(
    Z,
    o_ref,
    st_ref,
    wo_ref,
    first_ref,
    second_ref,
    far,
    far_st,
    near,
    near_st,
    pair,
    pair_st,
    both,
    both_st,
    cb,
    cb_st,
    rb,
    rb_st,
    wo_all,
    ctx,
    pb,
    pc,
    mm,
    pm,
    ph,
    ob,
    of,
    ring_send,
    ring_recv,
    x_send,
    x_recv,
    xs_send,
    xs_recv,
    b_send,
    b_recv,
    bs_send,
    bs_recv,
    c_send,
    c_recv,
    d_send,
    d_recv,
    y_send,
    y_recv,
    e_send,
    e_recv,
    local_sem,
):
    seq, head, z, x, at = place(Z)
    requests = o_ref.shape[0]
    heads = o_ref.shape[4] // HD
    span = requests // 2
    ys = Z // 2
    core, y = lax.rem(head, 2), head // 2
    partner = (seq, head + 1 - 2 * core)

    def along_y(d):
        return (seq, lax.rem(y + d, ys) * 2 + core)

    kept = pltpu.make_async_copy(wo_ref, wo_all.at[z // 2, lax.rem(z, 2)], local_sem.at[0])
    kept.start()
    greet(
        [at(d, 0) for d in range(1, Z)]
        + [at(0, d) for d in range(1, X)]
        + [along_y(d) for d in range(1, ys)]
        + [partner]
    )

    def far_off(i):
        return Z // 2 + (1 - 2 * lax.rem(i, 2)) * ((i + 1) // 2)

    def chunk(i):
        return lax.rem(z + far_off(i), Z), 1 - 2 * lax.rem(i, 2)

    def step_x(n):
        return lax.rem(x + n + X, X)

    def rows_of(half):
        return pl.ds(half * span, span)

    def send(kind, half, i, src, dst, table_src, table_dst, target):
        copies = [remote(src, dst, x_send.at[kind, half, i], x_recv.at[kind, half, i], target)]
        if half == 0:
            copies.append(remote(table_src, table_dst, xs_send.at[kind, i], xs_recv.at[kind, i], target))
        return copies

    def send_far(half, i):
        there, way = chunk(i)
        to = step_x(2)
        src = o_ref.at[rows_of(half), there, to]
        return send(0, half, i, src, far.at[half, there], st_ref.at[there, to], far_st.at[there], at(0, way + X))

    def send_near(half, i):
        there, way = chunk(i)
        to = step_x(-way)
        src = o_ref.at[rows_of(half), there, to]
        return send(1, half, i, src, near.at[half, there], st_ref.at[there, to], near_st.at[there], at(0, X - way))

    def send_pair(half, i):
        there, way = chunk(i)
        src, dst = pair.at[half, there], both.at[half, there]
        return send(2, half, i, src, dst, pair_st.at[there], both_st.at[there], at(0, way + X))

    def send_z(half, i):
        there, _ = chunk(i)
        target = (there * X + x, head)
        copies = [remote(cb.at[half, there], rb.at[half, i], b_send.at[half, i], b_recv.at[half, i], target)]
        if half == 0:
            copies.append(remote(cb_st.at[there], rb_st.at[i], bs_send.at[i], bs_recv.at[i], target))
        return copies

    def ring(right, k, src=None):
        block = lax.rem(z - k + Z, Z) if right else lax.rem(z + k, Z)
        way = 1 if right else 0
        slot = wo_all.at[block // 2, lax.rem(block, 2)]
        return remote(
            slot if src is None else src,
            slot,
            ring_send.at[way, k],
            ring_recv.at[way, k],
            at(1 if right else -1, 0),
        )

    right_steps, left_steps = Z // 2, Z - 1 - Z // 2

    def begin(half, i):
        for copy in send_far(half, i) + send_near(half, i):
            copy.start()

    for i in range(WINDOW + 1):
        begin(0, i)
    ring(True, 0, wo_ref).start()
    ring(False, 0, wo_ref).start()
    kept.wait()

    def middle(half, i):
        there, way = chunk(i)
        for copy in send_far(half, i):
            copy.wait_recv()
        table, factors = join([st_ref[there, step_x(way)], far_st[there]])
        if half == 0:
            pair_st[there] = table
        for r in range(span):
            sources = [o_ref[half * span + r, there, step_x(way)], far[half, there, r]]
            for h in range(heads):
                value = weigh(factors, sources, half * span + r, h)
                pair[half, there, r, :, h * HD : (h + 1) * HD] = value.astype(BF16)
        for copy in send_pair(half, i):
            copy.start()

    def end(half, i):
        there, _ = chunk(i)
        for copy in send_near(half, i) + send_pair(half, i):
            copy.wait_recv()
        table, factors = join([st_ref[there, x], near_st[there], both_st[there]])
        if half == 0:
            cb_st[there] = table
        for r in range(span):
            sources = [o_ref[half * span + r, there, x], near[half, there, r], both[half, there, r]]
            for h in range(heads):
                value = weigh(factors, sources, half * span + r, h)
                cb[half, there, r, :, h * HD : (h + 1) * HD] = value.astype(BF16)

    def closing(half, i):
        end(half, i)

        @pl.when(i < Z - 1)
        def _():
            for copy in send_z(half, i):
                copy.start()

    middle(0, 0)

    @pl.loop(1, Z)
    def _(i):
        @pl.when(i + WINDOW < Z)
        def _():
            begin(0, i + WINDOW)

        @pl.when(i + WINDOW >= Z)
        def _():
            begin(1, i + WINDOW - Z)

        middle(0, i)

        @pl.when(i >= LAG)
        def _():
            closing(0, i - LAG)

        @pl.when(i < right_steps)
        def _():
            ring(True, i - 1).wait_recv()
            ring(True, i).start()

        @pl.when(i < left_steps)
        def _():
            ring(False, i - 1).wait_recv()
            ring(False, i).start()

    begin(1, WINDOW)
    middle(1, 0)
    closing(0, Z - LAG)

    def second(low, high):
        @pl.loop(low, high)
        def _(i):
            @pl.when(i + WINDOW < Z)
            def _():
                begin(1, i + WINDOW)

            middle(1, i)

            @pl.when(i < LAG)
            def _():
                closing(0, Z + i - LAG)

            @pl.when(i >= LAG)
            def _():
                closing(1, i - LAG)

    mine = pl.multiple_of(x * (16 * span), 16 * span)

    def share(half, d):
        rows = ctx.at[half, pl.ds(mine, 16 * span)]
        return remote(rows, rows, c_send.at[half, d - 1], c_recv.at[half, d - 1], at(0, d))

    def settle(half):
        for i in range(Z - 1):
            for copy in send_z(half, i):
                copy.wait_recv()
        table, factors = join([cb_st[z]] + [rb_st[i] for i in range(Z - 1)])
        inverse = 1.0 / table
        for r in range(span):
            sources = [cb[half, z, r]] + [rb[half, i, r] for i in range(Z - 1)]
            for h in range(heads):
                lane = (half * span + r) * 8 + h
                value = weigh(factors, sources, half * span + r, h) * inverse[:, lane + 4 : lane + 5]
                ctx[half, pl.ds(mine + r * 16, 16), h * HD : (h + 1) * HD] = value.astype(BF16)
        for d in (2, 1, 3):
            share(half, d).start()

    def multiply(half, c):
        weights = wo_all[:, c].reshape(ys * BLK, ctx.shape[2])
        result = lax.dot_general(weights, ctx[half], NT, preferred_element_type=F32)
        return result.reshape(ys, BLK, ctx.shape[1])

    def to_core(half, d):
        there = lax.rem(y + d, ys)
        return remote(pb.at[half, there], pc.at[half, there], d_send.at[half, d], d_recv.at[half, d], partner)

    def to_y(half, d):
        return remote(
            pm.at[half, d - 1], ph.at[half, d - 1], y_send.at[half, d - 1], y_recv.at[half, d - 1], along_y(d)
        )

    def outputs(half):
        for d in range(1, X):
            share(half, d).wait_recv()
        pb[half] = multiply(half, 1 - core).astype(BF16)
        for d in (2, 1, 3, 0):
            to_core(half, d).start()
        mm[half] = multiply(half, core)

    def spread(half):
        for d in (2, 1, 3):
            there = lax.rem(y + d, ys)
            to_core(half, d).wait_recv()
            pm[half, d - 1] = (mm[half, there] + pc[half, there].astype(F32)).astype(BF16)
            to_y(half, d).start()

    def total(half):
        to_core(half, 0).wait_recv()
        value = mm[half, y] + pc[half, y].astype(F32)
        for d in range(1, ys):
            to_y(half, d).wait_recv()
            value = value + ph[half, d - 1].astype(F32)
        return value

    for word in LATE:
        if word[0] == "x":
            second(int(word[1]), int(word[2]))
        elif word == "own":

            @pl.loop(Z - LAG, Z)
            def _(i):
                closing(1, i)

        elif word == "wo":
            ring(True, right_steps - 1).wait_recv()
            ring(False, left_steps - 1).wait_recv()
        else:
            {"c": settle, "m": outputs, "y": spread}[word[0]](int(word[1]))
    early, late = total(0), total(1)
    low = lax.broadcasted_iota(jnp.int32, (BLK, 128), 1) < 64
    for t in range(X // 2):
        a, b = early[:, t * 128 : (t + 1) * 128], late[:, t * 128 : (t + 1) * 128]
        ob[:, t * 256 : t * 256 + 128] = jnp.where(low, a, pltpu.roll(b, 64, 1)).astype(BF16)
        ob[:, t * 256 + 128 : t * 256 + 256] = jnp.where(low, pltpu.roll(a, 64, 1), b).astype(BF16)
    column = pl.multiple_of(x * 128, 128)
    block = pl.ds(pl.multiple_of(x * BLK, 32), BLK)

    def to_owner(d):
        there = pl.multiple_of(lax.rem(x + d, X) * 128, 128)
        return remote(ob.at[:, pl.ds(there, 128)], of.at[block], e_send.at[d - 1], e_recv.at[d - 1], at(0, d))

    for d in (2, 1, 3):
        to_owner(d).start()
    last = pltpu.make_async_copy(ob.at[:, pl.ds(column, 128)], of.at[block], local_sem.at[1])
    last.start()
    last.wait()
    for d in range(1, X):
        to_owner(d).wait_recv()
    result = jnp.transpose(of[...].astype(F32))
    for r in range(requests):
        first_ref[r] = result[r * 16 : r * 16 + 8].astype(BF16)
        second_ref[r] = result[r * 16 + 8 : r * 16 + 16].astype(BF16)

    for half in range(2):
        @pl.loop(0, Z)
        def _(i):
            for copy in send_far(half, i) + send_near(half, i) + send_pair(half, i):
                copy.wait_send()

        for i in range(Z - 1):
            for copy in send_z(half, i):
                copy.wait_send()
        for d in range(1, X):
            share(half, d).wait_send()
        for d in range(ys):
            to_core(half, d).wait_send()
        for d in range(1, ys):
            to_y(half, d).wait_send()
    for k in range(right_steps):
        ring(True, k).wait_send()
    for k in range(left_steps):
        ring(False, k).wait_send()
    for d in range(1, X):
        to_owner(d).wait_send()


def finish(Z, out, table, w_out, tokens):
    requests = out.shape[0]
    cols = out.shape[4]
    rows = requests * 16
    ys = Z // 2
    vmem = pl.BlockSpec(memory_space=pltpu.VMEM)
    hbm = pl.BlockSpec(memory_space=pltpu.HBM)
    dma = pltpu.SemaphoreType.DMA
    shape = jax.ShapeDtypeStruct((requests, tokens, X * BLK), BF16)
    chunks = pltpu.VMEM((2, Z, requests // 2, 16, cols), BF16)
    tables = pltpu.VMEM((Z, 16, 128), F32)
    return pl.pallas_call(
        functools.partial(finish_kernel, Z),
        name="finish",
        out_shape=(shape, shape),
        in_specs=[vmem, vmem, hbm],
        out_specs=(vmem, vmem),
        scratch_shapes=[
            chunks,
            tables,
            chunks,
            tables,
            chunks,
            tables,
            chunks,
            tables,
            chunks,
            tables,
            pltpu.VMEM((2, Z - 1, requests // 2, 16, cols), BF16),
            pltpu.VMEM((Z - 1, 16, 128), F32),
            pltpu.VMEM((ys, 2, BLK, cols), BF16),
            pltpu.VMEM((2, X * rows // 2, cols), BF16),
            pltpu.VMEM((2, ys, BLK, X * rows // 2), BF16),
            pltpu.VMEM((2, ys, BLK, X * rows // 2), BF16),
            pltpu.VMEM((2, ys, BLK, X * rows // 2), F32),
            pltpu.VMEM((2, ys - 1, BLK, X * rows // 2), BF16),
            pltpu.VMEM((2, ys - 1, BLK, X * rows // 2), BF16),
            pltpu.VMEM((BLK, X * rows), BF16),
            pltpu.VMEM((X * BLK, rows), BF16),
            dma((2, Z // 2)),
            dma((2, Z // 2)),
            dma((3, 2, Z)),
            dma((3, 2, Z)),
            dma((3, Z)),
            dma((3, Z)),
            dma((2, Z - 1)),
            dma((2, Z - 1)),
            dma((Z - 1,)),
            dma((Z - 1,)),
            dma((2, X - 1)),
            dma((2, X - 1)),
            dma((2, ys)),
            dma((2, ys)),
            dma((2, ys - 1)),
            dma((2, ys - 1)),
            dma((X - 1,)),
            dma((X - 1,)),
            dma((2,)),
        ],
        compiler_params=pltpu.CompilerParams(
            collective_id=1, has_side_effects=True, vmem_limit_bytes=20 << 20
        ),
    )(out, table, *in_hbm(w_out))


def per_device(
    Z,
    block_input,
    accepted,
    accept_mask,
    cache_lengths,
    page_table,
    norm_gain,
    w_query,
    w_key,
    w_value,
    w_out,
    key_cache,
    value_cache,
):
    seq = lax.axis_index("seq")
    requests, tokens, width = block_input.shape
    half = HD // 2
    frequency = 10000.0 ** (-(jnp.arange(half).astype(F32) * 2.0) / HD)
    positions = (
        cache_lengths[:, None] + seq * tokens + jnp.arange(tokens, dtype=jnp.int32)[None, :]
    ).astype(F32)
    angles = jnp.broadcast_to(positions[:, None, :, None] * frequency, (requests, 2, tokens, half))
    angles = angles.reshape(requests * 2 * tokens, half)
    cosine, sine = jnp.cos(angles), jnp.sin(angles)
    cosine = jnp.concatenate([cosine, cosine], axis=1)
    sine = jnp.concatenate([-sine, sine], axis=1)

    q_all, new_keys, new_values = project(
        Z,
        block_input,
        accepted,
        accept_mask,
        norm_gain.reshape(1, width),
        cosine,
        sine,
        w_query,
        w_key,
        w_value,
    )
    cols = q_all.shape[3]
    queries = Z * X * 16
    out, table = attend(
        (seq * key_cache.shape[0]).astype(jnp.int32).reshape(1),
        cache_lengths,
        page_table.reshape(-1, 128),
        q_all.reshape(requests, queries, cols),
        key_cache,
        value_cache,
        new_keys.reshape(requests, 16, cols),
        new_values.reshape(requests, 16, cols),
    )
    return finish(Z, out.reshape(requests, Z, X, 16, cols), table.reshape(Z, X, 16, 128), w_out, tokens)


def solution(mesh):
    placed = (
        P(None, "seq", None),
        P(None, "seq", None),
        P(None, "seq"),
        P(),
        P(),
        P(),
        P("seq", "head"),
        P("seq", "head"),
        P("seq", "head"),
        P("seq", "head"),
        P("seq", None, "head"),
        P("seq", None, "head"),
    )
    return jax.shard_map(
        functools.partial(per_device, mesh.shape["seq"] // X),
        mesh=mesh,
        in_specs=placed,
        out_specs=(P(None, "seq", "head"), P(None, "seq", "head")),
        check_vma=False,
    )
```

```python
import functools

import jax
import jax.numpy as jnp
from jax import lax
from jax.experimental import pallas as pl
from jax.experimental.pallas import tpu as pltpu
from jax.sharding import PartitionSpec as P

HD = 128
PAGE = 128
MAXP = 64
X = 4
BLK = 160
FIRST = 6
WINDOW = 4
LAG = 3
HOLD = 2
PARTS = 2
UNROLL = 4
PAIR = 2
COVER = 256
MESH = pl.DeviceIdType.MESH
F32 = jnp.float32
BF16 = jnp.bfloat16
NT = (((1,), (1,)), ((), ()))
TN = (((0,), (0,)), ((), ()))


def in_hbm(*arrays):
    return [pltpu.with_memory_space_constraint(array, pltpu.HBM) for array in arrays]


ORDER = (
    "q1", "q2", "k0", "tf", "q3", "k1", "v0", "th", "mq07", "q4", "mq78", "sq",
    "k2", "v1", "mk05", "cq", "p0", "k3", "v2", "rx", "p1", "p2", "k4", "mk58",
    "sk", "v3", "p3", "p4", "v4", "mv08", "sv", "p5", "p6", "p7", "p8", "p9",
    "ck", "cv",
)


LATE = ("x16", "c0", "x68", "own", "wo", "m0", "c1", "m1", "y0", "y1")


def place(Z):
    seq = lax.axis_index("seq")
    head = lax.axis_index("head")
    z, x = seq // X, lax.rem(seq, X)

    def at(dz, dx):
        return (lax.rem(z + dz + Z, Z) * X + lax.rem(x + dx, X), head)

    return seq, head, z, x, at


def greet(partners):
    barrier = pltpu.get_barrier_semaphore()
    for partner in partners:
        pl.semaphore_signal(barrier, inc=1, device_id=partner, device_id_type=MESH)
    pl.semaphore_wait(barrier, len(partners))


def remote(src, dst, send, recv, target):
    return pltpu.make_async_remote_copy(
        src_ref=src, dst_ref=dst, send_sem=send, recv_sem=recv, device_id=target, device_id_type=MESH
    )


def project_kernel(
    Z,
    x_hbm,
    a_hbm,
    mask_hbm,
    gain_hbm,
    cos_ref,
    sin_ref,
    wq_ref,
    wk_ref,
    wv_ref,
    q_all,
    kn_ref,
    vn_ref,
    xs,
    as_,
    mask_ref,
    gain,
    xn,
    xg,
    wb,
    acc,
    part,
    got,
    qloc,
    ring_send,
    ring_recv,
    tok_send,
    tok_recv,
    core_send,
    core_recv,
    part_send,
    part_recv,
    zq_send,
    zq_recv,
    xq_send,
    xq_recv,
    rx_send,
    rx_recv,
    local_sem,
):
    seq, head, z, x, at = place(Z)
    width = X * BLK
    off = pl.multiple_of(32 * x, 32)
    own = (wq_ref, wk_ref, wv_ref)
    half = xs.shape[0]
    core = lax.rem(head, 2)
    partner = (seq, head + 1 - 2 * core)
    ours = pl.ds(core * half, half)
    loads = [
        pltpu.make_async_copy(x_hbm.at[ours], xs, local_sem.at[0]),
        pltpu.make_async_copy(a_hbm.at[ours], as_, local_sem.at[1]),
        pltpu.make_async_copy(gain_hbm, gain, local_sem.at[2]),
        pltpu.make_async_copy(mask_hbm, mask_ref, local_sem.at[8]),
    ]
    for copy in loads:
        copy.start()
    kept = [pltpu.make_async_copy(own[t], wb.at[t, z, pl.ds(off, BLK)], local_sem.at[3 + t]) for t in range(3)]
    for copy in kept:
        copy.start()
    greet([at(d, 0) for d in range(1, Z)] + [at(0, d) for d in range(1, X)] + [partner])

    def ring(right, t, k, bit):
        block = lax.rem(z - k + Z, Z) if right else lax.rem(z + k, Z)
        size = BLK // PARTS
        slot = wb.at[t, block, pl.ds(pl.multiple_of(off + bit * size, 16), size)]
        src = own[t].at[pl.ds(bit * size, size)] if k == 0 else slot
        way = 1 if right else 0
        send, recv = ring_send.at[way, t, k, bit], ring_recv.at[way, t, k, bit]
        return remote(src, slot, send, recv, at(1 if right else -1, 0))

    def steps(t, right):
        return Z // 2 if right == (t % 2 == 0) else Z - 1 - Z // 2

    def advance(t, k):
        for bit in range(PARTS):
            for right in (True, False):
                if 0 < k <= steps(t, right):
                    ring(right, t, k - 1, bit).wait_recv()
                if k < steps(t, right):
                    ring(right, t, k, bit).start()

    advance(0, 0)
    for copy in loads:
        copy.wait()

    diagonal = lax.broadcasted_iota(jnp.int32, (8, 8), 0) == lax.broadcasted_iota(jnp.int32, (8, 8), 1)

    @pl.loop(0, half)
    def _(r):
        accept = mask_ref[pl.ds(core * half + r, 1), :].astype(F32)
        accept = jnp.sum(jnp.where(diagonal, accept, 0.0), axis=1, keepdims=True)
        first = xs[r].astype(F32)
        second = jnp.where(accept == 1.0, as_[r].astype(F32), first)
        both = jnp.concatenate([first, second], axis=0)
        inverse = lax.rsqrt(jnp.mean(both * both, axis=-1, keepdims=True) + 1e-05)
        normed = (both * inverse * gain[...]).astype(BF16)
        rows = pl.ds(pl.multiple_of(r * 16, 16), 16)
        for c in range(Z):
            xn[c, rows, :] = normed[:, c * width : (c + 1) * width]

    share = half * 16
    mine = pl.ds(pl.multiple_of(x * 128, 128), 128)

    def cover(there):
        return xn.at[:, :, pl.ds(pl.multiple_of(there * 128, 128), COVER)]

    def rows_of(source):
        return xg.at[:, pl.ds(pl.multiple_of(source * 128 + core * share, share), share)]

    def token(d):
        return remote(cover(lax.rem(x + d, X)), rows_of(x), tok_send.at[d - 1], tok_recv.at[d - 1], at(0, d))

    def across(d):
        slot = rows_of(lax.rem(x - d + X, X))
        return remote(cover(x) if d == 0 else slot, slot, core_send.at[d], core_recv.at[d], partner)

    for d in (2, 1, 3):
        token(d).start()
    across(0).start()
    own_tokens = pltpu.make_async_copy(cover(x), rows_of(x), local_sem.at[6])
    own_tokens.start()

    zero = jnp.zeros((32, wb.shape[3]), BF16)

    @pl.loop(0, Z)
    def _(c):
        for t in range(3):
            for j in range(3):
                stripe = pl.multiple_of(32 * lax.rem(x + 5 + j, 8), 32)
                wb[t, c, pl.ds(stripe, 32), :] = zero

    acc[...] = jnp.zeros_like(acc)
    def multiply(t, low, high):
        @pl.loop(low, high)
        def _(j):
            block = lax.rem(z + (1 - 2 * lax.rem(j, 2)) * ((j + 1) // 2) + Z, Z)
            acc[t] += jnp.dot(xg[block], wb[t, block], preferred_element_type=F32)

    def piece(t, d):
        return remote(
            part.at[t, d - 1], got.at[t, d - 1], part_send.at[t, d - 1], part_recv.at[t, d - 1], at(0, d)
        )

    def spread(t):
        for d in (2, 1, 3):
            there = lax.rem(x + d, X)
            part[t, d - 1] = acc[t, pl.ds(pl.multiple_of(there * 128, 128), 128), :].astype(BF16)
            piece(t, d).start()

    def collect(t):
        total = acc[t, mine, :]
        for d in range(1, X):
            piece(t, d).wait_recv()
            total = total + got[t, d - 1].astype(F32)
        return total

    def turn(rows):
        pieces = []
        for h in range(rows.shape[1] // HD):
            piece = rows[:, h * HD : (h + 1) * HD]
            pieces.append(piece * cos_ref[...] + pltpu.roll(piece, HD // 2, 1) * sin_ref[...])
        return jnp.concatenate(pieces, axis=1).astype(BF16)

    first = pl.ds(0, FIRST)
    rest = pl.ds(FIRST, qloc.shape[0] - FIRST)
    hops = {True: Z // 2, False: Z - 1 - Z // 2}

    def to_z(right, k):
        slot = q_all.at[first, (lax.rem(z - k + Z, Z) if right else lax.rem(z + k, Z)) * X + x]
        i = 1 if right else 0
        return remote(
            qloc.at[first] if k == 0 else slot,
            slot,
            zq_send.at[0, i, k],
            zq_recv.at[0, i, k],
            at(1 if right else -1, 0),
        )

    def to_x(dz, way):
        slot = q_all.at[first, lax.rem(z - dz + Z, Z) * X + x]
        i = (way + 1) // 2
        return remote(
            qloc.at[first] if dz == 0 else slot, slot, xq_send.at[i, 0, dz], xq_recv.at[i, 0, dz], at(0, way + X)
        )

    def onward(dz):
        way = 1 - 2 * (dz % 2)
        slot = q_all.at[first, lax.rem(z - dz + Z, Z) * X + lax.rem(x - way + X, X)]
        i = (way + 1) // 2
        return remote(slot, slot, xq_send.at[i, 1, dz], xq_recv.at[i, 1, dz], at(0, way + X))

    def rest_x(d):
        return remote(qloc.at[rest], q_all.at[rest, seq], rx_send.at[d - 1], rx_recv.at[d - 1], at(0, d))

    def rest_z(right, k):
        block = lax.rem(z - k + Z, Z) if right else lax.rem(z + k, Z)
        slot = q_all.at[rest, pl.ds(block * X, X)]
        i = 1 if right else 0
        return remote(slot, slot, zq_send.at[1, i, k], zq_recv.at[1, i, k], at(1 if right else -1, 0))

    def rest_step(right, k):
        if 0 < k <= hops[right]:
            rest_z(right, k - 1).wait_recv()
        if 0 <= k < hops[right]:
            rest_z(right, k).start()

    arrival = [0] + sorted(range(1, Z), key=lambda d: min(d, Z - d))

    def pass_on(low, high):
        for i in range(low, high):
            if i < Z:
                dz = arrival[i]
                if dz:
                    right = dz <= hops[True]
                    k = dz if right else Z - dz
                    to_z(right, k - 1).wait_recv()
                    if k < hops[right]:
                        to_z(right, k).start()
                    rest_step(right, k - 1)
                to_x(dz, 1).start()
                to_x(dz, -1).start()
            if i >= HOLD:
                dz = arrival[i - HOLD]
                to_x(dz, 1 - 2 * (dz % 2)).wait_recv()
                onward(dz).start()

    own_query = pltpu.make_async_copy(qloc, q_all.at[:, seq], local_sem.at[7])

    def forward_tokens():
        for d in (1, 3, 2):
            token(d).wait_recv()
            across(d).start()

    def have_tokens():
        own_tokens.wait()
        for copy in kept:
            copy.wait()
        for d in range(X):
            across(d).wait_recv()

    def query_ready():
        query = turn(collect(0))
        for r in range(qloc.shape[0]):
            qloc[r] = query[r * 16 : (r + 1) * 16]
        to_z(True, 0).start()
        to_z(False, 0).start()
        for d in (2, 1, 3):
            rest_x(d).start()
        own_query.start()

    def have_rest():
        own_query.wait()
        for d in range(1, X):
            rest_x(d).wait_recv()

    def key_ready():
        kn_ref[...] = turn(collect(1))

    def value_ready():
        vn_ref[...] = collect(2).astype(BF16)

    named = {
        "tf": forward_tokens,
        "th": have_tokens,
        "cq": query_ready,
        "rx": have_rest,
        "ck": key_ready,
        "cv": value_ready,
    }
    for word in ORDER:
        if word in named:
            named[word]()
        elif word[0] == "m":
            multiply("qkv".index(word[1]), int(word[2]), int(word[3]))
        elif word[0] == "s":
            spread("qkv".index(word[1]))
        elif word[0] == "p":
            pass_on(int(word[1]), int(word[1]) + 1)
        else:
            advance("qkv".index(word[0]), int(word[1]))
    rest_step(False, hops[False])
    rest_step(True, hops[True])

    for t in range(3):
        for right in (True, False):
            for k in range(steps(t, right)):
                for bit in range(PARTS):
                    ring(right, t, k, bit).wait_send()
        for d in range(1, X):
            piece(t, d).wait_send()
    for d in range(1, X):
        token(d).wait_send()
    for d in range(X):
        across(d).wait_send()
    for right in (True, False):
        for k in range(hops[right]):
            to_z(right, k).wait_send()
            rest_z(right, k).wait_send()
    for d in range(1, X):
        rest_x(d).wait_send()
    for dz in range(Z):
        forwarded = 1 - 2 * (dz % 2)
        to_x(dz, -forwarded).wait_recv()
        onward(dz).wait()
        to_x(dz, 1).wait_send()
        to_x(dz, -1).wait_send()


def project(Z, block_input, accepted, mask, gain, cosine, sine, w_query, w_key, w_value):
    requests, tokens, width = block_input.shape
    cols = w_query.shape[1]
    rows = requests * 16
    vmem = pl.BlockSpec(memory_space=pltpu.VMEM)
    hbm = pl.BlockSpec(memory_space=pltpu.HBM)
    dma = pltpu.SemaphoreType.DMA
    return pl.pallas_call(
        functools.partial(project_kernel, Z),
        name="project",
        out_shape=(
            jax.ShapeDtypeStruct((requests, Z * X, 16, cols), BF16),
            jax.ShapeDtypeStruct((rows, cols), BF16),
            jax.ShapeDtypeStruct((rows, cols), BF16),
        ),
        in_specs=[hbm, hbm, hbm, hbm, vmem, vmem, hbm, hbm, hbm],
        out_specs=(vmem, vmem, vmem),
        scratch_shapes=[
            pltpu.VMEM((requests // 2, tokens, width), BF16),
            pltpu.VMEM((requests // 2, tokens, width), BF16),
            pltpu.VMEM(mask.shape, jnp.int32),
            pltpu.VMEM((1, width), F32),
            pltpu.VMEM((Z, rows // 2, X * BLK), BF16),
            pltpu.VMEM((Z, X * rows, COVER), BF16),
            pltpu.VMEM((3, Z, COVER, cols), BF16),
            pltpu.VMEM((3, X * rows, cols), F32),
            pltpu.VMEM((3, X - 1, rows, cols), BF16),
            pltpu.VMEM((3, X - 1, rows, cols), BF16),
            pltpu.VMEM((requests, 16, cols), BF16),
            dma((2, 3, Z // 2, PARTS)),
            dma((2, 3, Z // 2, PARTS)),
            dma((X - 1,)),
            dma((X - 1,)),
            dma((X,)),
            dma((X,)),
            dma((3, X - 1)),
            dma((3, X - 1)),
            dma((2, 2, Z // 2)),
            dma((2, 2, Z // 2)),
            dma((2, 2, Z)),
            dma((2, 2, Z)),
            dma((X - 1,)),
            dma((X - 1,)),
            dma((9,)),
        ],
        compiler_params=pltpu.CompilerParams(
            collective_id=0, has_side_effects=True, vmem_limit_bytes=24 << 20
        ),
    )(*in_hbm(block_input, accepted, mask, gain), cosine, sine, *in_hbm(w_query, w_key, w_value))


def attend_kernel(
    base,
    lengths_hbm,
    table_hbm,
    q_ref,
    k_ref,
    v_hbm,
    kn_ref,
    vn_ref,
    o_ref,
    st_ref,
    acc,
    stats,
    qt,
    v_ref,
    table_ref,
    lengths,
    page,
    owner,
    live,
    sems,
):
    heads = acc.shape[1]
    queries = acc.shape[3]
    scale = HD ** (-0.5)
    loads = [
        pltpu.make_async_copy(lengths_hbm, lengths, sems.at[0]),
        pltpu.make_async_copy(table_hbm, table_ref, sems.at[1]),
        pltpu.make_async_copy(v_hbm, v_ref, sems.at[2]),
    ]
    for copy in loads:
        copy.start()
    stats[...] = jnp.zeros_like(stats)

    key_pass = lax.broadcasted_iota(jnp.int32, (16, queries), 0) // 8
    query_pass = lax.rem(lax.broadcasted_iota(jnp.int32, (16, queries), 1) // 8, 2)
    same = key_pass == query_pass

    def block_part(r):
        for h in range(heads):
            col = slice(h * HD, (h + 1) * HD)
            qt[r, h] = jnp.transpose(q_ref[r, :, col])
            scores = jnp.dot(kn_ref[r, :, col], qt[r, h], preferred_element_type=F32) * scale
            scores = jnp.where(same, scores, -1e30)
            peak = jnp.max(scores, axis=0, keepdims=True)
            weights = jnp.where(same, jnp.exp(scores - peak), 0.0)
            high = weights.astype(BF16)
            low = (weights - high.astype(F32)).astype(BF16)
            values = vn_ref[r, :, col]
            acc[r, h] = lax.dot_general(
                jnp.concatenate([values, values], axis=0),
                jnp.concatenate([high, low], axis=0),
                TN,
                preferred_element_type=F32,
            )
            stats[pl.ds(r * 8 + h, 1), :] = peak
            stats[pl.ds(r * 8 + 4 + h, 1), :] = jnp.sum(weights, axis=0, keepdims=True)

    @pl.loop(0, q_ref.shape[0] // UNROLL)
    def _(i):
        for j in range(UNROLL):
            block_part(i * UNROLL + j)

    for copy in loads:
        copy.wait()
    shape = table_ref.shape
    slots = lax.broadcasted_iota(jnp.int32, shape, 0) * shape[1] + lax.broadcasted_iota(jnp.int32, shape, 1)
    slots = slots.astype(F32)
    count = jnp.int32(0)
    for p in range(k_ref.shape[0]):
        found = jnp.sum(jnp.where(table_ref[...] == base[0] + p, slots, 0.0)).astype(jnp.int32)
        alive = lengths[found // MAXP] - lax.rem(found, MAXP) * PAGE
        page[count] = p
        owner[count] = found // MAXP
        live[count] = alive
        count = count + jnp.where(alive > 0, 1, 0)
    page[count] = 0
    owner[count] = 0
    live[count] = 0

    slot = lax.broadcasted_iota(jnp.int32, (PAGE, queries), 0)

    def page_part(n):
        p, r = page[n], owner[n]
        alive = slot < live[n]
        for h in range(heads):
            col = slice(h * HD, (h + 1) * HD)
            scores = jnp.dot(k_ref[p, :, col], qt[r, h], preferred_element_type=F32) * scale
            scores = jnp.where(alive, scores, -1e30)
            page_peak = jnp.max(scores, axis=0, keepdims=True)
            weights = jnp.exp(scores - page_peak)
            page_out = lax.dot_general(v_ref[p, :, col], weights.astype(BF16), TN, preferred_element_type=F32)
            m_row = pl.ds(r * 8 + h, 1)
            l_row = pl.ds(r * 8 + 4 + h, 1)
            before = stats[m_row, :]
            after = jnp.maximum(before, page_peak)
            old, new = jnp.exp(before - after), jnp.exp(page_peak - after)
            acc[r, h] = acc[r, h] * old + page_out * new
            stats[m_row, :] = after
            stats[l_row, :] = stats[l_row, :] * old + jnp.sum(weights, axis=0, keepdims=True) * new

    @pl.loop(0, (count + PAIR - 1) // PAIR)
    def _(i):
        for j in range(PAIR):
            page_part(i * PAIR + j)

    @pl.loop(0, q_ref.shape[0])
    def _(r):
        for h in range(heads):
            o_ref[r, :, h * HD : (h + 1) * HD] = jnp.transpose(acc[r, h].astype(BF16))

    st_ref[...] = jnp.transpose(stats[...])


def attend(base, lengths, page_table, q_all, key_cache, value_cache, new_keys, new_values):
    requests, queries, cols = q_all.shape
    pages = key_cache.shape[0]
    heads = cols // HD
    vmem = pl.BlockSpec(memory_space=pltpu.VMEM)
    smem = pl.BlockSpec(memory_space=pltpu.SMEM)
    hbm = pl.BlockSpec(memory_space=pltpu.HBM)
    return pl.pallas_call(
        attend_kernel,
        name="attend",
        out_shape=(
            jax.ShapeDtypeStruct((requests, queries, cols), BF16),
            jax.ShapeDtypeStruct((queries, 128), F32),
        ),
        in_specs=[smem, hbm, hbm, vmem, vmem, hbm, vmem, vmem],
        out_specs=(vmem, vmem),
        scratch_shapes=[
            pltpu.VMEM((requests, heads, HD, queries), F32),
            pltpu.VMEM((128, queries), F32),
            pltpu.VMEM((requests, heads, HD, queries), BF16),
            pltpu.VMEM(value_cache.shape, BF16),
            pltpu.VMEM(page_table.shape, jnp.int32),
            pltpu.SMEM(lengths.shape, jnp.int32),
            pltpu.SMEM((pages + 1,), jnp.int32),
            pltpu.SMEM((pages + 1,), jnp.int32),
            pltpu.SMEM((pages + 1,), jnp.int32),
            pltpu.SemaphoreType.DMA((3,)),
        ],
        compiler_params=pltpu.CompilerParams(vmem_limit_bytes=20 << 20),
    )(base, *in_hbm(lengths, page_table), q_all, key_cache, *in_hbm(value_cache), new_keys, new_values)


def join(tables):
    peak = functools.reduce(jnp.maximum, tables)
    factors = [jnp.exp(table - peak) for table in tables]
    total = sum(pltpu.roll(factor, 4, 1) * table for factor, table in zip(factors, tables))
    lane = lax.broadcasted_iota(jnp.int32, peak.shape, 1)
    return jnp.where(lax.rem(lane, 8) >= 4, total, peak), factors


def weigh(factors, sources, r, h):
    lane = r * 8 + h
    return sum(
        factor[:, lane : lane + 1] * source[:, h * HD : (h + 1) * HD].astype(F32)
        for factor, source in zip(factors, sources)
    )


def finish_kernel(
    Z,
    o_ref,
    st_ref,
    wo_ref,
    first_ref,
    second_ref,
    far,
    far_st,
    near,
    near_st,
    pair,
    pair_st,
    both,
    both_st,
    cb,
    cb_st,
    rb,
    rb_st,
    wo_all,
    ctx,
    pb,
    pc,
    mm,
    pm,
    ph,
    ob,
    of,
    ring_send,
    ring_recv,
    x_send,
    x_recv,
    xs_send,
    xs_recv,
    b_send,
    b_recv,
    bs_send,
    bs_recv,
    c_send,
    c_recv,
    d_send,
    d_recv,
    y_send,
    y_recv,
    e_send,
    e_recv,
    local_sem,
):
    seq, head, z, x, at = place(Z)
    requests = o_ref.shape[0]
    heads = o_ref.shape[4] // HD
    span = requests // 2
    ys = Z // 2
    core, y = lax.rem(head, 2), head // 2
    partner = (seq, head + 1 - 2 * core)

    def along_y(d):
        return (seq, lax.rem(y + d, ys) * 2 + core)

    kept = pltpu.make_async_copy(wo_ref, wo_all.at[z // 2, lax.rem(z, 2)], local_sem.at[0])
    kept.start()
    greet(
        [at(d, 0) for d in range(1, Z)]
        + [at(0, d) for d in range(1, X)]
        + [along_y(d) for d in range(1, ys)]
        + [partner]
    )

    def far_off(i):
        return Z // 2 + (1 - 2 * lax.rem(i, 2)) * ((i + 1) // 2)

    def chunk(i):
        return lax.rem(z + far_off(i), Z), 1 - 2 * lax.rem(i, 2)

    def step_x(n):
        return lax.rem(x + n + X, X)

    def rows_of(half):
        return pl.ds(half * span, span)

    def send(kind, half, i, src, dst, table_src, table_dst, target):
        copies = [remote(src, dst, x_send.at[kind, half, i], x_recv.at[kind, half, i], target)]
        if half == 0:
            copies.append(remote(table_src, table_dst, xs_send.at[kind, i], xs_recv.at[kind, i], target))
        return copies

    def send_far(half, i):
        there, way = chunk(i)
        to = step_x(2)
        src = o_ref.at[rows_of(half), there, to]
        return send(0, half, i, src, far.at[half, there], st_ref.at[there, to], far_st.at[there], at(0, way + X))

    def send_near(half, i):
        there, way = chunk(i)
        to = step_x(-way)
        src = o_ref.at[rows_of(half), there, to]
        return send(1, half, i, src, near.at[half, there], st_ref.at[there, to], near_st.at[there], at(0, X - way))

    def send_pair(half, i):
        there, way = chunk(i)
        src, dst = pair.at[half, there], both.at[half, there]
        return send(2, half, i, src, dst, pair_st.at[there], both_st.at[there], at(0, way + X))

    def send_z(half, i):
        there, _ = chunk(i)
        target = (there * X + x, head)
        copies = [remote(cb.at[half, there], rb.at[half, i], b_send.at[half, i], b_recv.at[half, i], target)]
        if half == 0:
            copies.append(remote(cb_st.at[there], rb_st.at[i], bs_send.at[i], bs_recv.at[i], target))
        return copies

    def ring(right, k, src=None):
        block = lax.rem(z - k + Z, Z) if right else lax.rem(z + k, Z)
        way = 1 if right else 0
        slot = wo_all.at[block // 2, lax.rem(block, 2)]
        return remote(
            slot if src is None else src,
            slot,
            ring_send.at[way, k],
            ring_recv.at[way, k],
            at(1 if right else -1, 0),
        )

    right_steps, left_steps = Z // 2, Z - 1 - Z // 2

    def begin(half, i):
        for copy in send_far(half, i) + send_near(half, i):
            copy.start()

    for i in range(WINDOW + 1):
        begin(0, i)
    ring(True, 0, wo_ref).start()
    ring(False, 0, wo_ref).start()
    kept.wait()

    def middle(half, i):
        there, way = chunk(i)
        for copy in send_far(half, i):
            copy.wait_recv()
        table, factors = join([st_ref[there, step_x(way)], far_st[there]])
        if half == 0:
            pair_st[there] = table
        for r in range(span):
            sources = [o_ref[half * span + r, there, step_x(way)], far[half, there, r]]
            for h in range(heads):
                value = weigh(factors, sources, half * span + r, h)
                pair[half, there, r, :, h * HD : (h + 1) * HD] = value.astype(BF16)
        for copy in send_pair(half, i):
            copy.start()

    def end(half, i):
        there, _ = chunk(i)
        for copy in send_near(half, i) + send_pair(half, i):
            copy.wait_recv()
        table, factors = join([st_ref[there, x], near_st[there], both_st[there]])
        if half == 0:
            cb_st[there] = table
        for r in range(span):
            sources = [o_ref[half * span + r, there, x], near[half, there, r], both[half, there, r]]
            for h in range(heads):
                value = weigh(factors, sources, half * span + r, h)
                cb[half, there, r, :, h * HD : (h + 1) * HD] = value.astype(BF16)

    def closing(half, i):
        end(half, i)

        @pl.when(i < Z - 1)
        def _():
            for copy in send_z(half, i):
                copy.start()

    middle(0, 0)

    @pl.loop(1, Z)
    def _(i):
        @pl.when(i + WINDOW < Z)
        def _():
            begin(0, i + WINDOW)

        @pl.when(i + WINDOW >= Z)
        def _():
            begin(1, i + WINDOW - Z)

        middle(0, i)

        @pl.when(i >= LAG)
        def _():
            closing(0, i - LAG)

        @pl.when(i < right_steps)
        def _():
            ring(True, i - 1).wait_recv()
            ring(True, i).start()

        @pl.when(i < left_steps)
        def _():
            ring(False, i - 1).wait_recv()
            ring(False, i).start()

    begin(1, WINDOW)
    middle(1, 0)
    closing(0, Z - LAG)

    def second(low, high):
        @pl.loop(low, high)
        def _(i):
            @pl.when(i + WINDOW < Z)
            def _():
                begin(1, i + WINDOW)

            middle(1, i)

            @pl.when(i < LAG)
            def _():
                closing(0, Z + i - LAG)

            @pl.when(i >= LAG)
            def _():
                closing(1, i - LAG)

    mine = pl.multiple_of(x * (16 * span), 16 * span)

    def share(half, d):
        rows = ctx.at[half, pl.ds(mine, 16 * span)]
        return remote(rows, rows, c_send.at[half, d - 1], c_recv.at[half, d - 1], at(0, d))

    def settle(half):
        for i in range(Z - 1):
            for copy in send_z(half, i):
                copy.wait_recv()
        table, factors = join([cb_st[z]] + [rb_st[i] for i in range(Z - 1)])
        inverse = 1.0 / table
        for r in range(span):
            sources = [cb[half, z, r]] + [rb[half, i, r] for i in range(Z - 1)]
            for h in range(heads):
                lane = (half * span + r) * 8 + h
                value = weigh(factors, sources, half * span + r, h) * inverse[:, lane + 4 : lane + 5]
                ctx[half, pl.ds(mine + r * 16, 16), h * HD : (h + 1) * HD] = value.astype(BF16)
        for d in (2, 1, 3):
            share(half, d).start()

    def multiply(half, c):
        weights = wo_all[:, c].reshape(ys * BLK, ctx.shape[2])
        result = lax.dot_general(weights, ctx[half], NT, preferred_element_type=F32)
        return result.reshape(ys, BLK, ctx.shape[1])

    def to_core(half, d):
        there = lax.rem(y + d, ys)
        return remote(pb.at[half, there], pc.at[half, there], d_send.at[half, d], d_recv.at[half, d], partner)

    def to_y(half, d):
        return remote(
            pm.at[half, d - 1], ph.at[half, d - 1], y_send.at[half, d - 1], y_recv.at[half, d - 1], along_y(d)
        )

    def outputs(half):
        for d in range(1, X):
            share(half, d).wait_recv()
        pb[half] = multiply(half, 1 - core).astype(BF16)
        for d in (2, 1, 3, 0):
            to_core(half, d).start()
        mm[half] = multiply(half, core)

    def spread(half):
        for d in (2, 1, 3):
            there = lax.rem(y + d, ys)
            to_core(half, d).wait_recv()
            pm[half, d - 1] = (mm[half, there] + pc[half, there].astype(F32)).astype(BF16)
            to_y(half, d).start()

    def total(half):
        to_core(half, 0).wait_recv()
        value = mm[half, y] + pc[half, y].astype(F32)
        for d in range(1, ys):
            to_y(half, d).wait_recv()
            value = value + ph[half, d - 1].astype(F32)
        return value

    for word in LATE:
        if word[0] == "x":
            second(int(word[1]), int(word[2]))
        elif word == "own":

            @pl.loop(Z - LAG, Z)
            def _(i):
                closing(1, i)

        elif word == "wo":
            ring(True, right_steps - 1).wait_recv()
            ring(False, left_steps - 1).wait_recv()
        else:
            {"c": settle, "m": outputs, "y": spread}[word[0]](int(word[1]))
    early, late = total(0), total(1)
    low = lax.broadcasted_iota(jnp.int32, (BLK, 128), 1) < 64
    for t in range(X // 2):
        a, b = early[:, t * 128 : (t + 1) * 128], late[:, t * 128 : (t + 1) * 128]
        ob[:, t * 256 : t * 256 + 128] = jnp.where(low, a, pltpu.roll(b, 64, 1)).astype(BF16)
        ob[:, t * 256 + 128 : t * 256 + 256] = jnp.where(low, pltpu.roll(a, 64, 1), b).astype(BF16)
    column = pl.multiple_of(x * 128, 128)
    block = pl.ds(pl.multiple_of(x * BLK, 32), BLK)

    def to_owner(d):
        there = pl.multiple_of(lax.rem(x + d, X) * 128, 128)
        return remote(ob.at[:, pl.ds(there, 128)], of.at[block], e_send.at[d - 1], e_recv.at[d - 1], at(0, d))

    for d in (2, 1, 3):
        to_owner(d).start()
    last = pltpu.make_async_copy(ob.at[:, pl.ds(column, 128)], of.at[block], local_sem.at[1])
    last.start()
    last.wait()
    for d in range(1, X):
        to_owner(d).wait_recv()
    result = jnp.transpose(of[...].astype(F32))
    for r in range(requests):
        first_ref[r] = result[r * 16 : r * 16 + 8].astype(BF16)
        second_ref[r] = result[r * 16 + 8 : r * 16 + 16].astype(BF16)

    for half in range(2):
        @pl.loop(0, Z)
        def _(i):
            for copy in send_far(half, i) + send_near(half, i) + send_pair(half, i):
                copy.wait_send()

        for i in range(Z - 1):
            for copy in send_z(half, i):
                copy.wait_send()
        for d in range(1, X):
            share(half, d).wait_send()
        for d in range(ys):
            to_core(half, d).wait_send()
        for d in range(1, ys):
            to_y(half, d).wait_send()
    for k in range(right_steps):
        ring(True, k).wait_send()
    for k in range(left_steps):
        ring(False, k).wait_send()
    for d in range(1, X):
        to_owner(d).wait_send()


def finish(Z, out, table, w_out, tokens):
    requests = out.shape[0]
    cols = out.shape[4]
    rows = requests * 16
    ys = Z // 2
    vmem = pl.BlockSpec(memory_space=pltpu.VMEM)
    hbm = pl.BlockSpec(memory_space=pltpu.HBM)
    dma = pltpu.SemaphoreType.DMA
    shape = jax.ShapeDtypeStruct((requests, tokens, X * BLK), BF16)
    chunks = pltpu.VMEM((2, Z, requests // 2, 16, cols), BF16)
    tables = pltpu.VMEM((Z, 16, 128), F32)
    return pl.pallas_call(
        functools.partial(finish_kernel, Z),
        name="finish",
        out_shape=(shape, shape),
        in_specs=[vmem, vmem, hbm],
        out_specs=(vmem, vmem),
        scratch_shapes=[
            chunks,
            tables,
            chunks,
            tables,
            chunks,
            tables,
            chunks,
            tables,
            chunks,
            tables,
            pltpu.VMEM((2, Z - 1, requests // 2, 16, cols), BF16),
            pltpu.VMEM((Z - 1, 16, 128), F32),
            pltpu.VMEM((ys, 2, BLK, cols), BF16),
            pltpu.VMEM((2, X * rows // 2, cols), BF16),
            pltpu.VMEM((2, ys, BLK, X * rows // 2), BF16),
            pltpu.VMEM((2, ys, BLK, X * rows // 2), BF16),
            pltpu.VMEM((2, ys, BLK, X * rows // 2), F32),
            pltpu.VMEM((2, ys - 1, BLK, X * rows // 2), BF16),
            pltpu.VMEM((2, ys - 1, BLK, X * rows // 2), BF16),
            pltpu.VMEM((BLK, X * rows), BF16),
            pltpu.VMEM((X * BLK, rows), BF16),
            dma((2, Z // 2)),
            dma((2, Z // 2)),
            dma((3, 2, Z)),
            dma((3, 2, Z)),
            dma((3, Z)),
            dma((3, Z)),
            dma((2, Z - 1)),
            dma((2, Z - 1)),
            dma((Z - 1,)),
            dma((Z - 1,)),
            dma((2, X - 1)),
            dma((2, X - 1)),
            dma((2, ys)),
            dma((2, ys)),
            dma((2, ys - 1)),
            dma((2, ys - 1)),
            dma((X - 1,)),
            dma((X - 1,)),
            dma((2,)),
        ],
        compiler_params=pltpu.CompilerParams(
            collective_id=1, has_side_effects=True, vmem_limit_bytes=20 << 20
        ),
    )(out, table, *in_hbm(w_out))


def per_device(
    Z,
    block_input,
    accepted,
    accept_mask,
    cache_lengths,
    page_table,
    norm_gain,
    w_query,
    w_key,
    w_value,
    w_out,
    key_cache,
    value_cache,
):
    seq = lax.axis_index("seq")
    requests, tokens, width = block_input.shape
    half = HD // 2
    frequency = 10000.0 ** (-(jnp.arange(half).astype(F32) * 2.0) / HD)
    positions = (
        cache_lengths[:, None] + seq * tokens + jnp.arange(tokens, dtype=jnp.int32)[None, :]
    ).astype(F32)
    angles = jnp.broadcast_to(positions[:, None, :, None] * frequency, (requests, 2, tokens, half))
    angles = angles.reshape(requests * 2 * tokens, half)
    cosine, sine = jnp.cos(angles), jnp.sin(angles)
    cosine = jnp.concatenate([cosine, cosine], axis=1)
    sine = jnp.concatenate([-sine, sine], axis=1)

    q_all, new_keys, new_values = project(
        Z,
        block_input,
        accepted,
        accept_mask,
        norm_gain.reshape(1, width),
        cosine,
        sine,
        w_query,
        w_key,
        w_value,
    )
    cols = q_all.shape[3]
    queries = Z * X * 16
    out, table = attend(
        (seq * key_cache.shape[0]).astype(jnp.int32).reshape(1),
        cache_lengths,
        page_table.reshape(-1, 128),
        q_all.reshape(requests, queries, cols),
        key_cache,
        value_cache,
        new_keys.reshape(requests, 16, cols),
        new_values.reshape(requests, 16, cols),
    )
    return finish(Z, out.reshape(requests, Z, X, 16, cols), table.reshape(Z, X, 16, 128), w_out, tokens)


def solution(mesh):
    placed = (
        P(None, "seq", None),
        P(None, "seq", None),
        P(None, "seq"),
        P(),
        P(),
        P(),
        P("seq", "head"),
        P("seq", "head"),
        P("seq", "head"),
        P("seq", "head"),
        P("seq", None, "head"),
        P("seq", None, "head"),
    )
    return jax.shard_map(
        functools.partial(per_device, mesh.shape["seq"] // X),
        mesh=mesh,
        in_specs=placed,
        out_specs=(P(None, "seq", "head"), P(None, "seq", "head")),
        check_vma=False,
    )
```

```python
import functools

import jax
import jax.numpy as jnp
from jax import lax
from jax.experimental import pallas as pl
from jax.experimental.pallas import tpu as pltpu
from jax.sharding import PartitionSpec as P

HD = 128
PAGE = 128
MAXP = 64
X = 4
BLK = 160
FIRST = 6
WINDOW = 4
LAG = 3
HOLD = 2
PARTS = 2
UNROLL = 4
PAIR = 2
COVER = 256
MESH = pl.DeviceIdType.MESH
F32 = jnp.float32
BF16 = jnp.bfloat16
NT = (((1,), (1,)), ((), ()))
TN = (((0,), (0,)), ((), ()))


def in_hbm(*arrays):
    return [pltpu.with_memory_space_constraint(array, pltpu.HBM) for array in arrays]


ORDER = (
    "q1", "q2", "k0", "tf", "q3", "k1", "v0", "th", "mq07", "q4", "mq78", "sq",
    "k2", "v1", "mk05", "cq", "p0", "k3", "v2", "rx", "p1", "p2", "k4", "mk58",
    "sk", "v3", "p3", "jk", "p4", "v4", "mv08", "sv", "p5", "p6", "jv", "p7",
    "p8", "p9", "ck", "cv",
)

LATE = ("x16", "c0", "x68", "own", "wo", "m0", "c1", "m1", "y0", "y1")


def place(Z):
    seq = lax.axis_index("seq")
    head = lax.axis_index("head")
    z, x = seq // X, lax.rem(seq, X)

    def at(dz, dx):
        return (lax.rem(z + dz + Z, Z) * X + lax.rem(x + dx, X), head)

    return seq, head, z, x, at


def greet(partners):
    barrier = pltpu.get_barrier_semaphore()
    for partner in partners:
        pl.semaphore_signal(barrier, inc=1, device_id=partner, device_id_type=MESH)
    pl.semaphore_wait(barrier, len(partners))


def remote(src, dst, send, recv, target):
    return pltpu.make_async_remote_copy(
        src_ref=src, dst_ref=dst, send_sem=send, recv_sem=recv, device_id=target, device_id_type=MESH
    )


def project_kernel(
    Z,
    x_hbm,
    a_hbm,
    mask_hbm,
    gain_hbm,
    cos_ref,
    sin_ref,
    wq_ref,
    wk_ref,
    wv_ref,
    q_all,
    kn_ref,
    vn_ref,
    xs,
    as_,
    mask_ref,
    gain,
    xn,
    xg,
    wb,
    acc,
    part,
    got,
    qloc,
    ring_send,
    ring_recv,
    tok_send,
    tok_recv,
    core_send,
    core_recv,
    part_send,
    part_recv,
    zq_send,
    zq_recv,
    xq_send,
    xq_recv,
    rx_send,
    rx_recv,
    local_sem,
):
    seq, head, z, x, at = place(Z)
    width = X * BLK
    off = pl.multiple_of(32 * x, 32)
    own = (wq_ref, wk_ref, wv_ref)
    half = xs.shape[0]
    core = lax.rem(head, 2)
    partner = (seq, head + 1 - 2 * core)
    ours = pl.ds(core * half, half)
    loads = [
        pltpu.make_async_copy(x_hbm.at[ours], xs, local_sem.at[0]),
        pltpu.make_async_copy(a_hbm.at[ours], as_, local_sem.at[1]),
        pltpu.make_async_copy(gain_hbm, gain, local_sem.at[2]),
        pltpu.make_async_copy(mask_hbm, mask_ref, local_sem.at[8]),
    ]
    for copy in loads:
        copy.start()
    kept = [pltpu.make_async_copy(own[t], wb.at[t, z, pl.ds(off, BLK)], local_sem.at[3 + t]) for t in range(3)]
    for copy in kept:
        copy.start()
    greet([at(d, 0) for d in range(1, Z)] + [at(0, d) for d in range(1, X)] + [partner])

    def ring(right, t, k, bit):
        block = lax.rem(z - k + Z, Z) if right else lax.rem(z + k, Z)
        size = BLK // PARTS
        slot = wb.at[t, block, pl.ds(pl.multiple_of(off + bit * size, 16), size)]
        src = own[t].at[pl.ds(bit * size, size)] if k == 0 else slot
        way = 1 if right else 0
        send, recv = ring_send.at[way, t, k, bit], ring_recv.at[way, t, k, bit]
        return remote(src, slot, send, recv, at(1 if right else -1, 0))

    def steps(t, right):
        return Z // 2 if right == (t % 2 == 0) else Z - 1 - Z // 2

    def advance(t, k):
        for bit in range(PARTS):
            for right in (True, False):
                if 0 < k <= steps(t, right):
                    ring(right, t, k - 1, bit).wait_recv()
                if k < steps(t, right):
                    ring(right, t, k, bit).start()

    advance(0, 0)
    for copy in loads:
        copy.wait()

    diagonal = lax.broadcasted_iota(jnp.int32, (8, 8), 0) == lax.broadcasted_iota(jnp.int32, (8, 8), 1)

    @pl.loop(0, half)
    def _(r):
        accept = mask_ref[pl.ds(core * half + r, 1), :].astype(F32)
        accept = jnp.sum(jnp.where(diagonal, accept, 0.0), axis=1, keepdims=True)
        first = xs[r].astype(F32)
        second = jnp.where(accept == 1.0, as_[r].astype(F32), first)
        both = jnp.concatenate([first, second], axis=0)
        inverse = lax.rsqrt(jnp.mean(both * both, axis=-1, keepdims=True) + 1e-05)
        normed = (both * inverse * gain[...]).astype(BF16)
        rows = pl.ds(pl.multiple_of(r * 16, 16), 16)
        for c in range(Z):
            xn[c, rows, :] = normed[:, c * width : (c + 1) * width]

    share = half * 16
    mine = pl.ds(pl.multiple_of(x * 128, 128), 128)

    def cover(there):
        return xn.at[:, :, pl.ds(pl.multiple_of(there * 128, 128), COVER)]

    def rows_of(source):
        return xg.at[:, pl.ds(pl.multiple_of(source * 128 + core * share, share), share)]

    def token(d):
        return remote(cover(lax.rem(x + d, X)), rows_of(x), tok_send.at[d - 1], tok_recv.at[d - 1], at(0, d))

    def across(d):
        slot = rows_of(lax.rem(x - d + X, X))
        return remote(cover(x) if d == 0 else slot, slot, core_send.at[d], core_recv.at[d], partner)

    for d in (2, 1, 3):
        token(d).start()
    across(0).start()
    own_tokens = pltpu.make_async_copy(cover(x), rows_of(x), local_sem.at[6])
    own_tokens.start()

    zero = jnp.zeros((32, wb.shape[3]), BF16)

    @pl.loop(0, Z)
    def _(c):
        for t in range(3):
            for j in range(3):
                stripe = pl.multiple_of(32 * lax.rem(x + 5 + j, 8), 32)
                wb[t, c, pl.ds(stripe, 32), :] = zero

    acc[...] = jnp.zeros_like(acc)
    def multiply(t, low, high):
        @pl.loop(low, high)
        def _(j):
            block = lax.rem(z + (1 - 2 * lax.rem(j, 2)) * ((j + 1) // 2) + Z, Z)
            acc[t] += jnp.dot(xg[block], wb[t, block], preferred_element_type=F32)

    def piece(t, d):
        return remote(
            part.at[t, d - 1], got.at[t, d - 1], part_send.at[t, d - 1], part_recv.at[t, d - 1], at(0, d)
        )

    def spread(t):
        for d in (2, 1, 3):
            there = lax.rem(x + d, X)
            part[t, d - 1] = acc[t, pl.ds(pl.multiple_of(there * 128, 128), 128), :].astype(BF16)
            piece(t, d).start()

    def rows_at(n):
        return pl.ds(pl.multiple_of(lax.rem(x + n + X, X) * 128, 128), 128)

    def relay(t, kind):
        way = 1 if t == 1 else -1
        target = at(0, X - way) if kind == 0 else at(0, X + way)
        return remote(part.at[t, kind], got.at[t, kind], part_send.at[t, kind], part_recv.at[t, kind], target)

    def spread_two(t):
        way = 1 if t == 1 else -1
        part[t, 1] = acc[t, rows_at(2), :].astype(BF16)
        relay(t, 1).start()
        part[t, 0] = acc[t, rows_at(-way), :].astype(BF16)
        relay(t, 0).start()

    def join_two(t):
        way = 1 if t == 1 else -1
        relay(t, 1).wait_recv()
        part[t, 2] = (acc[t, rows_at(way), :] + got[t, 1].astype(F32)).astype(BF16)
        relay(t, 2).start()

    def collect_two(t):
        relay(t, 0).wait_recv()
        relay(t, 2).wait_recv()
        return acc[t, mine, :] + got[t, 0].astype(F32) + got[t, 2].astype(F32)

    def collect(t):
        total = acc[t, mine, :]
        for d in range(1, X):
            piece(t, d).wait_recv()
            total = total + got[t, d - 1].astype(F32)
        return total

    def turn(rows):
        pieces = []
        for h in range(rows.shape[1] // HD):
            piece = rows[:, h * HD : (h + 1) * HD]
            pieces.append(piece * cos_ref[...] + pltpu.roll(piece, HD // 2, 1) * sin_ref[...])
        return jnp.concatenate(pieces, axis=1).astype(BF16)

    first = pl.ds(0, FIRST)
    rest = pl.ds(FIRST, qloc.shape[0] - FIRST)
    hops = {True: Z // 2, False: Z - 1 - Z // 2}

    def to_z(right, k):
        slot = q_all.at[first, (lax.rem(z - k + Z, Z) if right else lax.rem(z + k, Z)) * X + x]
        i = 1 if right else 0
        return remote(
            qloc.at[first] if k == 0 else slot,
            slot,
            zq_send.at[0, i, k],
            zq_recv.at[0, i, k],
            at(1 if right else -1, 0),
        )

    def to_x(dz, way):
        slot = q_all.at[first, lax.rem(z - dz + Z, Z) * X + x]
        i = (way + 1) // 2
        return remote(
            qloc.at[first] if dz == 0 else slot, slot, xq_send.at[i, 0, dz], xq_recv.at[i, 0, dz], at(0, way + X)
        )

    def onward(dz):
        way = 1 - 2 * (dz % 2)
        slot = q_all.at[first, lax.rem(z - dz + Z, Z) * X + lax.rem(x - way + X, X)]
        i = (way + 1) // 2
        return remote(slot, slot, xq_send.at[i, 1, dz], xq_recv.at[i, 1, dz], at(0, way + X))

    def rest_x(d):
        return remote(qloc.at[rest], q_all.at[rest, seq], rx_send.at[d - 1], rx_recv.at[d - 1], at(0, d))

    def rest_z(right, k):
        block = lax.rem(z - k + Z, Z) if right else lax.rem(z + k, Z)
        slot = q_all.at[rest, pl.ds(block * X, X)]
        i = 1 if right else 0
        return remote(slot, slot, zq_send.at[1, i, k], zq_recv.at[1, i, k], at(1 if right else -1, 0))

    def rest_step(right, k):
        if 0 < k <= hops[right]:
            rest_z(right, k - 1).wait_recv()
        if 0 <= k < hops[right]:
            rest_z(right, k).start()

    arrival = [0] + sorted(range(1, Z), key=lambda d: min(d, Z - d))

    def pass_on(low, high):
        for i in range(low, high):
            if i < Z:
                dz = arrival[i]
                if dz:
                    right = dz <= hops[True]
                    k = dz if right else Z - dz
                    to_z(right, k - 1).wait_recv()
                    if k < hops[right]:
                        to_z(right, k).start()
                    rest_step(right, k - 1)
                to_x(dz, 1).start()
                to_x(dz, -1).start()
            if i >= HOLD:
                dz = arrival[i - HOLD]
                to_x(dz, 1 - 2 * (dz % 2)).wait_recv()
                onward(dz).start()

    own_query = pltpu.make_async_copy(qloc, q_all.at[:, seq], local_sem.at[7])

    def forward_tokens():
        for d in (1, 3, 2):
            token(d).wait_recv()
            across(d).start()

    def have_tokens():
        own_tokens.wait()
        for copy in kept:
            copy.wait()
        for d in range(X):
            across(d).wait_recv()

    def query_ready():
        query = turn(collect(0))
        for r in range(qloc.shape[0]):
            qloc[r] = query[r * 16 : (r + 1) * 16]
        to_z(True, 0).start()
        to_z(False, 0).start()
        for d in (2, 1, 3):
            rest_x(d).start()
        own_query.start()

    def have_rest():
        own_query.wait()
        for d in range(1, X):
            rest_x(d).wait_recv()

    def key_ready():
        kn_ref[...] = turn(collect_two(1))

    def value_ready():
        vn_ref[...] = collect_two(2).astype(BF16)

    named = {
        "tf": forward_tokens,
        "th": have_tokens,
        "cq": query_ready,
        "rx": have_rest,
        "ck": key_ready,
        "cv": value_ready,
    }
    for word in ORDER:
        if word in named:
            named[word]()
        elif word[0] == "m":
            multiply("qkv".index(word[1]), int(word[2]), int(word[3]))
        elif word == "sq":
            spread(0)
        elif word[0] == "s":
            spread_two("qkv".index(word[1]))
        elif word[0] == "j":
            join_two("qkv".index(word[1]))
        elif word[0] == "p":
            pass_on(int(word[1]), int(word[1]) + 1)
        else:
            advance("qkv".index(word[0]), int(word[1]))
    rest_step(False, hops[False])
    rest_step(True, hops[True])

    for t in range(3):
        for right in (True, False):
            for k in range(steps(t, right)):
                for bit in range(PARTS):
                    ring(right, t, k, bit).wait_send()
        for d in range(1, X):
            (piece(t, d) if t == 0 else relay(t, d - 1)).wait_send()
    for d in range(1, X):
        token(d).wait_send()
    for d in range(X):
        across(d).wait_send()
    for right in (True, False):
        for k in range(hops[right]):
            to_z(right, k).wait_send()
            rest_z(right, k).wait_send()
    for d in range(1, X):
        rest_x(d).wait_send()
    for dz in range(Z):
        forwarded = 1 - 2 * (dz % 2)
        to_x(dz, -forwarded).wait_recv()
        onward(dz).wait()
        to_x(dz, 1).wait_send()
        to_x(dz, -1).wait_send()


def project(Z, block_input, accepted, mask, gain, cosine, sine, w_query, w_key, w_value):
    requests, tokens, width = block_input.shape
    cols = w_query.shape[1]
    rows = requests * 16
    vmem = pl.BlockSpec(memory_space=pltpu.VMEM)
    hbm = pl.BlockSpec(memory_space=pltpu.HBM)
    dma = pltpu.SemaphoreType.DMA
    return pl.pallas_call(
        functools.partial(project_kernel, Z),
        name="project",
        out_shape=(
            jax.ShapeDtypeStruct((requests, Z * X, 16, cols), BF16),
            jax.ShapeDtypeStruct((rows, cols), BF16),
            jax.ShapeDtypeStruct((rows, cols), BF16),
        ),
        in_specs=[hbm, hbm, hbm, hbm, vmem, vmem, hbm, hbm, hbm],
        out_specs=(vmem, vmem, vmem),
        scratch_shapes=[
            pltpu.VMEM((requests // 2, tokens, width), BF16),
            pltpu.VMEM((requests // 2, tokens, width), BF16),
            pltpu.VMEM(mask.shape, jnp.int32),
            pltpu.VMEM((1, width), F32),
            pltpu.VMEM((Z, rows // 2, X * BLK), BF16),
            pltpu.VMEM((Z, X * rows, COVER), BF16),
            pltpu.VMEM((3, Z, COVER, cols), BF16),
            pltpu.VMEM((3, X * rows, cols), F32),
            pltpu.VMEM((3, X - 1, rows, cols), BF16),
            pltpu.VMEM((3, X - 1, rows, cols), BF16),
            pltpu.VMEM((requests, 16, cols), BF16),
            dma((2, 3, Z // 2, PARTS)),
            dma((2, 3, Z // 2, PARTS)),
            dma((X - 1,)),
            dma((X - 1,)),
            dma((X,)),
            dma((X,)),
            dma((3, X - 1)),
            dma((3, X - 1)),
            dma((2, 2, Z // 2)),
            dma((2, 2, Z // 2)),
            dma((2, 2, Z)),
            dma((2, 2, Z)),
            dma((X - 1,)),
            dma((X - 1,)),
            dma((9,)),
        ],
        compiler_params=pltpu.CompilerParams(
            collective_id=0, has_side_effects=True, vmem_limit_bytes=24 << 20
        ),
    )(*in_hbm(block_input, accepted, mask, gain), cosine, sine, *in_hbm(w_query, w_key, w_value))


def attend_kernel(
    base,
    lengths_hbm,
    table_hbm,
    q_ref,
    k_ref,
    v_hbm,
    kn_ref,
    vn_ref,
    o_ref,
    st_ref,
    acc,
    stats,
    qt,
    v_ref,
    table_ref,
    lengths,
    page,
    owner,
    live,
    sems,
):
    heads = acc.shape[1]
    queries = acc.shape[3]
    scale = HD ** (-0.5)
    loads = [
        pltpu.make_async_copy(lengths_hbm, lengths, sems.at[0]),
        pltpu.make_async_copy(table_hbm, table_ref, sems.at[1]),
        pltpu.make_async_copy(v_hbm, v_ref, sems.at[2]),
    ]
    for copy in loads:
        copy.start()
    stats[...] = jnp.zeros_like(stats)

    key_pass = lax.broadcasted_iota(jnp.int32, (16, queries), 0) // 8
    query_pass = lax.rem(lax.broadcasted_iota(jnp.int32, (16, queries), 1) // 8, 2)
    same = key_pass == query_pass

    def block_part(r):
        for h in range(heads):
            col = slice(h * HD, (h + 1) * HD)
            qt[r, h] = jnp.transpose(q_ref[r, :, col])
            scores = jnp.dot(kn_ref[r, :, col], qt[r, h], preferred_element_type=F32) * scale
            scores = jnp.where(same, scores, -1e30)
            peak = jnp.max(scores, axis=0, keepdims=True)
            weights = jnp.where(same, jnp.exp(scores - peak), 0.0)
            high = weights.astype(BF16)
            low = (weights - high.astype(F32)).astype(BF16)
            values = vn_ref[r, :, col]
            acc[r, h] = lax.dot_general(
                jnp.concatenate([values, values], axis=0),
                jnp.concatenate([high, low], axis=0),
                TN,
                preferred_element_type=F32,
            )
            stats[pl.ds(r * 8 + h, 1), :] = peak
            stats[pl.ds(r * 8 + 4 + h, 1), :] = jnp.sum(weights, axis=0, keepdims=True)

    @pl.loop(0, q_ref.shape[0] // UNROLL)
    def _(i):
        for j in range(UNROLL):
            block_part(i * UNROLL + j)

    for copy in loads:
        copy.wait()
    shape = table_ref.shape
    slots = lax.broadcasted_iota(jnp.int32, shape, 0) * shape[1] + lax.broadcasted_iota(jnp.int32, shape, 1)
    slots = slots.astype(F32)
    count = jnp.int32(0)
    for p in range(k_ref.shape[0]):
        found = jnp.sum(jnp.where(table_ref[...] == base[0] + p, slots, 0.0)).astype(jnp.int32)
        alive = lengths[found // MAXP] - lax.rem(found, MAXP) * PAGE
        page[count] = p
        owner[count] = found // MAXP
        live[count] = alive
        count = count + jnp.where(alive > 0, 1, 0)
    page[count] = 0
    owner[count] = 0
    live[count] = 0

    slot = lax.broadcasted_iota(jnp.int32, (PAGE, queries), 0)

    def page_part(n):
        p, r = page[n], owner[n]
        alive = slot < live[n]
        for h in range(heads):
            col = slice(h * HD, (h + 1) * HD)
            scores = jnp.dot(k_ref[p, :, col], qt[r, h], preferred_element_type=F32) * scale
            scores = jnp.where(alive, scores, -1e30)
            page_peak = jnp.max(scores, axis=0, keepdims=True)
            weights = jnp.exp(scores - page_peak)
            page_out = lax.dot_general(v_ref[p, :, col], weights.astype(BF16), TN, preferred_element_type=F32)
            m_row = pl.ds(r * 8 + h, 1)
            l_row = pl.ds(r * 8 + 4 + h, 1)
            before = stats[m_row, :]
            after = jnp.maximum(before, page_peak)
            old, new = jnp.exp(before - after), jnp.exp(page_peak - after)
            acc[r, h] = acc[r, h] * old + page_out * new
            stats[m_row, :] = after
            stats[l_row, :] = stats[l_row, :] * old + jnp.sum(weights, axis=0, keepdims=True) * new

    @pl.loop(0, (count + PAIR - 1) // PAIR)
    def _(i):
        for j in range(PAIR):
            page_part(i * PAIR + j)

    @pl.loop(0, q_ref.shape[0] // UNROLL)
    def _(i):
        for j in range(UNROLL):
            r = i * UNROLL + j
            for h in range(heads):
                o_ref[r, :, h * HD : (h + 1) * HD] = jnp.transpose(acc[r, h].astype(BF16))

    rows = jnp.transpose(stats[...]).reshape(queries // 16, 16, 128)
    st_ref[...] = rows[:, :8] + pltpu.roll(rows[:, 8:], 64, 2)


def attend(base, lengths, page_table, q_all, key_cache, value_cache, new_keys, new_values):
    requests, queries, cols = q_all.shape
    pages = key_cache.shape[0]
    heads = cols // HD
    vmem = pl.BlockSpec(memory_space=pltpu.VMEM)
    smem = pl.BlockSpec(memory_space=pltpu.SMEM)
    hbm = pl.BlockSpec(memory_space=pltpu.HBM)
    return pl.pallas_call(
        attend_kernel,
        name="attend",
        out_shape=(
            jax.ShapeDtypeStruct((requests, queries, cols), BF16),
            jax.ShapeDtypeStruct((queries // 16, 8, 128), F32),
        ),
        in_specs=[smem, hbm, hbm, vmem, vmem, hbm, vmem, vmem],
        out_specs=(vmem, vmem),
        scratch_shapes=[
            pltpu.VMEM((requests, heads, HD, queries), F32),
            pltpu.VMEM((128, queries), F32),
            pltpu.VMEM((requests, heads, HD, queries), BF16),
            pltpu.VMEM(value_cache.shape, BF16),
            pltpu.VMEM(page_table.shape, jnp.int32),
            pltpu.SMEM(lengths.shape, jnp.int32),
            pltpu.SMEM((pages + 1,), jnp.int32),
            pltpu.SMEM((pages + 1,), jnp.int32),
            pltpu.SMEM((pages + 1,), jnp.int32),
            pltpu.SemaphoreType.DMA((3,)),
        ],
        compiler_params=pltpu.CompilerParams(vmem_limit_bytes=20 << 20),
    )(base, *in_hbm(lengths, page_table), q_all, key_cache, *in_hbm(value_cache), new_keys, new_values)


def join(tables):
    peak = functools.reduce(jnp.maximum, tables)
    factors = [jnp.exp(table - peak) for table in tables]
    total = sum(pltpu.roll(factor, 4, 1) * table for factor, table in zip(factors, tables))
    lane = lax.broadcasted_iota(jnp.int32, peak.shape, 1)
    return jnp.where(lax.rem(lane, 8) >= 4, total, peak), factors


def per_row(table, lane):
    return jnp.concatenate([table[:, lane : lane + 1], table[:, lane + 64 : lane + 65]], axis=0)


def weigh(factors, sources, r, h):
    lane = r * 8 + h
    return sum(
        per_row(factor, lane) * source[:, h * HD : (h + 1) * HD].astype(F32)
        for factor, source in zip(factors, sources)
    )


def finish_kernel(
    Z,
    o_ref,
    st_ref,
    wo_ref,
    first_ref,
    second_ref,
    far,
    far_st,
    near,
    near_st,
    pair,
    pair_st,
    both,
    both_st,
    cb,
    cb_st,
    rb,
    rb_st,
    wo_all,
    ctx,
    pb,
    pc,
    mm,
    pm,
    ph,
    ob,
    of,
    ring_send,
    ring_recv,
    x_send,
    x_recv,
    xs_send,
    xs_recv,
    b_send,
    b_recv,
    bs_send,
    bs_recv,
    c_send,
    c_recv,
    d_send,
    d_recv,
    y_send,
    y_recv,
    e_send,
    e_recv,
    local_sem,
):
    seq, head, z, x, at = place(Z)
    requests = o_ref.shape[0]
    heads = o_ref.shape[4] // HD
    span = requests // 2
    ys = Z // 2
    core, y = lax.rem(head, 2), head // 2
    partner = (seq, head + 1 - 2 * core)

    def along_y(d):
        return (seq, lax.rem(y + d, ys) * 2 + core)

    kept = pltpu.make_async_copy(wo_ref, wo_all.at[z // 2, lax.rem(z, 2)], local_sem.at[0])
    kept.start()
    greet(
        [at(d, 0) for d in range(1, Z)]
        + [at(0, d) for d in range(1, X)]
        + [along_y(d) for d in range(1, ys)]
        + [partner]
    )

    def far_off(i):
        return Z // 2 + (1 - 2 * lax.rem(i, 2)) * ((i + 1) // 2)

    def chunk(i):
        return lax.rem(z + far_off(i), Z), 1 - 2 * lax.rem(i, 2)

    def step_x(n):
        return lax.rem(x + n + X, X)

    def rows_of(half):
        return pl.ds(half * span, span)

    def send(kind, half, i, src, dst, table_src, table_dst, target):
        copies = [remote(src, dst, x_send.at[kind, half, i], x_recv.at[kind, half, i], target)]
        if half == 0:
            copies.append(remote(table_src, table_dst, xs_send.at[kind, i], xs_recv.at[kind, i], target))
        return copies

    def send_far(half, i):
        there, way = chunk(i)
        to = step_x(2)
        src = o_ref.at[rows_of(half), there, to]
        return send(0, half, i, src, far.at[half, there], st_ref.at[there, to], far_st.at[there], at(0, way + X))

    def send_near(half, i):
        there, way = chunk(i)
        to = step_x(-way)
        src = o_ref.at[rows_of(half), there, to]
        return send(1, half, i, src, near.at[half, there], st_ref.at[there, to], near_st.at[there], at(0, X - way))

    def send_pair(half, i):
        there, way = chunk(i)
        src, dst = pair.at[half, there], both.at[half, there]
        return send(2, half, i, src, dst, pair_st.at[there], both_st.at[there], at(0, way + X))

    def send_z(half, i):
        there, _ = chunk(i)
        target = (there * X + x, head)
        copies = [remote(cb.at[half, there], rb.at[half, i], b_send.at[half, i], b_recv.at[half, i], target)]
        if half == 0:
            copies.append(remote(cb_st.at[there], rb_st.at[i], bs_send.at[i], bs_recv.at[i], target))
        return copies

    def ring(right, k, src=None):
        block = lax.rem(z - k + Z, Z) if right else lax.rem(z + k, Z)
        way = 1 if right else 0
        slot = wo_all.at[block // 2, lax.rem(block, 2)]
        return remote(
            slot if src is None else src,
            slot,
            ring_send.at[way, k],
            ring_recv.at[way, k],
            at(1 if right else -1, 0),
        )

    right_steps, left_steps = Z // 2, Z - 1 - Z // 2

    def begin(half, i):
        for copy in send_far(half, i) + send_near(half, i):
            copy.start()

    for i in range(WINDOW + 1):
        begin(0, i)
    ring(True, 0, wo_ref).start()
    ring(False, 0, wo_ref).start()
    kept.wait()

    def middle(half, i):
        there, way = chunk(i)
        for copy in send_far(half, i):
            copy.wait_recv()
        table, factors = join([st_ref[there, step_x(way)], far_st[there]])
        if half == 0:
            pair_st[there] = table
        for r in range(span):
            sources = [o_ref[half * span + r, there, step_x(way)], far[half, there, r]]
            for h in range(heads):
                value = weigh(factors, sources, half * span + r, h)
                pair[half, there, r, :, h * HD : (h + 1) * HD] = value.astype(BF16)
        for copy in send_pair(half, i):
            copy.start()

    def end(half, i):
        there, _ = chunk(i)
        for copy in send_near(half, i) + send_pair(half, i):
            copy.wait_recv()
        table, factors = join([st_ref[there, x], near_st[there], both_st[there]])
        if half == 0:
            cb_st[there] = table
        for r in range(span):
            sources = [o_ref[half * span + r, there, x], near[half, there, r], both[half, there, r]]
            for h in range(heads):
                value = weigh(factors, sources, half * span + r, h)
                cb[half, there, r, :, h * HD : (h + 1) * HD] = value.astype(BF16)

    def closing(half, i):
        end(half, i)

        @pl.when(i < Z - 1)
        def _():
            for copy in send_z(half, i):
                copy.start()

    middle(0, 0)

    @pl.loop(1, Z)
    def _(i):
        @pl.when(i + WINDOW < Z)
        def _():
            begin(0, i + WINDOW)

        @pl.when(i + WINDOW >= Z)
        def _():
            begin(1, i + WINDOW - Z)

        middle(0, i)

        @pl.when(i >= LAG)
        def _():
            closing(0, i - LAG)

        @pl.when(i < right_steps)
        def _():
            ring(True, i - 1).wait_recv()
            ring(True, i).start()

        @pl.when(i < left_steps)
        def _():
            ring(False, i - 1).wait_recv()
            ring(False, i).start()

    begin(1, WINDOW)
    middle(1, 0)
    closing(0, Z - LAG)

    def second(low, high):
        @pl.loop(low, high)
        def _(i):
            @pl.when(i + WINDOW < Z)
            def _():
                begin(1, i + WINDOW)

            middle(1, i)

            @pl.when(i < LAG)
            def _():
                closing(0, Z + i - LAG)

            @pl.when(i >= LAG)
            def _():
                closing(1, i - LAG)

    mine = pl.multiple_of(x * (16 * span), 16 * span)

    def share(half, d):
        rows = ctx.at[half, pl.ds(mine, 16 * span)]
        return remote(rows, rows, c_send.at[half, d - 1], c_recv.at[half, d - 1], at(0, d))

    def settle(half):
        for i in range(Z - 1):
            for copy in send_z(half, i):
                copy.wait_recv()
        table, factors = join([cb_st[z]] + [rb_st[i] for i in range(Z - 1)])
        inverse = 1.0 / table
        for r in range(span):
            sources = [cb[half, z, r]] + [rb[half, i, r] for i in range(Z - 1)]
            for h in range(heads):
                lane = (half * span + r) * 8 + h
                value = weigh(factors, sources, half * span + r, h) * per_row(inverse, lane + 4)
                ctx[half, pl.ds(mine + r * 16, 16), h * HD : (h + 1) * HD] = value.astype(BF16)
        for d in (2, 1, 3):
            share(half, d).start()

    def multiply(half, c):
        weights = wo_all[:, c].reshape(ys * BLK, ctx.shape[2])
        result = lax.dot_general(weights, ctx[half], NT, preferred_element_type=F32)
        return result.reshape(ys, BLK, ctx.shape[1])

    def to_core(half, d):
        there = lax.rem(y + d, ys)
        return remote(pb.at[half, there], pc.at[half, there], d_send.at[half, d], d_recv.at[half, d], partner)

    def to_y(half, d):
        return remote(
            pm.at[half, d - 1], ph.at[half, d - 1], y_send.at[half, d - 1], y_recv.at[half, d - 1], along_y(d)
        )

    def outputs(half):
        for d in range(1, X):
            share(half, d).wait_recv()
        pb[half] = multiply(half, 1 - core).astype(BF16)
        for d in (2, 1, 3, 0):
            to_core(half, d).start()
        mm[half] = multiply(half, core)

    def spread(half):
        for d in (2, 1, 3):
            there = lax.rem(y + d, ys)
            to_core(half, d).wait_recv()
            pm[half, d - 1] = (mm[half, there] + pc[half, there].astype(F32)).astype(BF16)
            to_y(half, d).start()

    def total(half):
        to_core(half, 0).wait_recv()
        value = mm[half, y] + pc[half, y].astype(F32)
        for d in range(1, ys):
            to_y(half, d).wait_recv()
            value = value + ph[half, d - 1].astype(F32)
        return value

    for word in LATE:
        if word[0] == "x":
            second(int(word[1]), int(word[2]))
        elif word == "own":

            @pl.loop(Z - LAG, Z)
            def _(i):
                closing(1, i)

        elif word == "wo":
            ring(True, right_steps - 1).wait_recv()
            ring(False, left_steps - 1).wait_recv()
        else:
            {"c": settle, "m": outputs, "y": spread}[word[0]](int(word[1]))
    early, late = total(0), total(1)
    low = lax.broadcasted_iota(jnp.int32, (BLK, 128), 1) < 64
    for t in range(X // 2):
        a, b = early[:, t * 128 : (t + 1) * 128], late[:, t * 128 : (t + 1) * 128]
        ob[:, t * 256 : t * 256 + 128] = jnp.where(low, a, pltpu.roll(b, 64, 1)).astype(BF16)
        ob[:, t * 256 + 128 : t * 256 + 256] = jnp.where(low, pltpu.roll(a, 64, 1), b).astype(BF16)
    column = pl.multiple_of(x * 128, 128)
    block = pl.ds(pl.multiple_of(x * BLK, 32), BLK)

    def to_owner(d):
        there = pl.multiple_of(lax.rem(x + d, X) * 128, 128)
        return remote(ob.at[:, pl.ds(there, 128)], of.at[block], e_send.at[d - 1], e_recv.at[d - 1], at(0, d))

    for d in (2, 1, 3):
        to_owner(d).start()
    last = pltpu.make_async_copy(ob.at[:, pl.ds(column, 128)], of.at[block], local_sem.at[1])
    last.start()
    last.wait()
    for d in range(1, X):
        to_owner(d).wait_recv()
    result = jnp.transpose(of[...].astype(F32))
    for r in range(requests):
        first_ref[r] = result[r * 16 : r * 16 + 8].astype(BF16)
        second_ref[r] = result[r * 16 + 8 : r * 16 + 16].astype(BF16)

    for half in range(2):
        @pl.loop(0, Z)
        def _(i):
            for copy in send_far(half, i) + send_near(half, i) + send_pair(half, i):
                copy.wait_send()

        for i in range(Z - 1):
            for copy in send_z(half, i):
                copy.wait_send()
        for d in range(1, X):
            share(half, d).wait_send()
        for d in range(ys):
            to_core(half, d).wait_send()
        for d in range(1, ys):
            to_y(half, d).wait_send()
    for k in range(right_steps):
        ring(True, k).wait_send()
    for k in range(left_steps):
        ring(False, k).wait_send()
    for d in range(1, X):
        to_owner(d).wait_send()


def finish(Z, out, table, w_out, tokens):
    requests = out.shape[0]
    cols = out.shape[4]
    rows = requests * 16
    ys = Z // 2
    vmem = pl.BlockSpec(memory_space=pltpu.VMEM)
    hbm = pl.BlockSpec(memory_space=pltpu.HBM)
    dma = pltpu.SemaphoreType.DMA
    shape = jax.ShapeDtypeStruct((requests, tokens, X * BLK), BF16)
    chunks = pltpu.VMEM((2, Z, requests // 2, 16, cols), BF16)
    tables = pltpu.VMEM((Z, 8, 128), F32)
    return pl.pallas_call(
        functools.partial(finish_kernel, Z),
        name="finish",
        out_shape=(shape, shape),
        in_specs=[vmem, vmem, hbm],
        out_specs=(vmem, vmem),
        scratch_shapes=[
            chunks,
            tables,
            chunks,
            tables,
            chunks,
            tables,
            chunks,
            tables,
            chunks,
            tables,
            pltpu.VMEM((2, Z - 1, requests // 2, 16, cols), BF16),
            pltpu.VMEM((Z - 1, 8, 128), F32),
            pltpu.VMEM((ys, 2, BLK, cols), BF16),
            pltpu.VMEM((2, X * rows // 2, cols), BF16),
            pltpu.VMEM((2, ys, BLK, X * rows // 2), BF16),
            pltpu.VMEM((2, ys, BLK, X * rows // 2), BF16),
            pltpu.VMEM((2, ys, BLK, X * rows // 2), F32),
            pltpu.VMEM((2, ys - 1, BLK, X * rows // 2), BF16),
            pltpu.VMEM((2, ys - 1, BLK, X * rows // 2), BF16),
            pltpu.VMEM((BLK, X * rows), BF16),
            pltpu.VMEM((X * BLK, rows), BF16),
            dma((2, Z // 2)),
            dma((2, Z // 2)),
            dma((3, 2, Z)),
            dma((3, 2, Z)),
            dma((3, Z)),
            dma((3, Z)),
            dma((2, Z - 1)),
            dma((2, Z - 1)),
            dma((Z - 1,)),
            dma((Z - 1,)),
            dma((2, X - 1)),
            dma((2, X - 1)),
            dma((2, ys)),
            dma((2, ys)),
            dma((2, ys - 1)),
            dma((2, ys - 1)),
            dma((X - 1,)),
            dma((X - 1,)),
            dma((2,)),
        ],
        compiler_params=pltpu.CompilerParams(
            collective_id=1, has_side_effects=True, vmem_limit_bytes=20 << 20
        ),
    )(out, table, *in_hbm(w_out))


def per_device(
    Z,
    block_input,
    accepted,
    accept_mask,
    cache_lengths,
    page_table,
    norm_gain,
    w_query,
    w_key,
    w_value,
    w_out,
    key_cache,
    value_cache,
):
    seq = lax.axis_index("seq")
    requests, tokens, width = block_input.shape
    half = HD // 2
    frequency = 10000.0 ** (-(jnp.arange(half).astype(F32) * 2.0) / HD)
    positions = (
        cache_lengths[:, None] + seq * tokens + jnp.arange(tokens, dtype=jnp.int32)[None, :]
    ).astype(F32)
    angles = jnp.broadcast_to(positions[:, None, :, None] * frequency, (requests, 2, tokens, half))
    angles = angles.reshape(requests * 2 * tokens, half)
    cosine, sine = jnp.cos(angles), jnp.sin(angles)
    cosine = jnp.concatenate([cosine, cosine], axis=1)
    sine = jnp.concatenate([-sine, sine], axis=1)

    q_all, new_keys, new_values = project(
        Z,
        block_input,
        accepted,
        accept_mask,
        norm_gain.reshape(1, width),
        cosine,
        sine,
        w_query,
        w_key,
        w_value,
    )
    cols = q_all.shape[3]
    queries = Z * X * 16
    out, table = attend(
        (seq * key_cache.shape[0]).astype(jnp.int32).reshape(1),
        cache_lengths,
        page_table.reshape(-1, 128),
        q_all.reshape(requests, queries, cols),
        key_cache,
        value_cache,
        new_keys.reshape(requests, 16, cols),
        new_values.reshape(requests, 16, cols),
    )
    return finish(Z, out.reshape(requests, Z, X, 16, cols), table.reshape(Z, X, 8, 128), w_out, tokens)


def solution(mesh):
    placed = (
        P(None, "seq", None),
        P(None, "seq", None),
        P(None, "seq"),
        P(),
        P(),
        P(),
        P("seq", "head"),
        P("seq", "head"),
        P("seq", "head"),
        P("seq", "head"),
        P("seq", None, "head"),
        P("seq", None, "head"),
    )
    return jax.shard_map(
        functools.partial(per_device, mesh.shape["seq"] // X),
        mesh=mesh,
        in_specs=placed,
        out_specs=(P(None, "seq", "head"), P(None, "seq", "head")),
        check_vma=False,
    )
```
